32 devices in a mesh: groups: 2 (over x), lat: 16 (over z, y, core).
Axes of the slice: x: 2, y: 2, z: 4, core: 2. Of those that a mesh axis runs over, the one named last changes fastest.
Arguments:
- harmonic_right_sides: float32 [16, 8, 2, 640, 640], P('groups', None, None, 'lat'), parts along dimension 0, may hold values from -0.625 to 0.625
- azimuthal_number_list: int32 [640], replicated, may hold values from 0 to 639, each once
- parallel_arrangement: int32 [160], replicated, may hold values from 0 to 159, each once
- polar_basis_values: bfloat16 [640, 160, 640], P('lat'), may hold values from -0.25 to 0.25
- eigen_forward_matrix: float32 [8, 8], replicated, may hold values from -2 to 2
- eigen_back_matrix: float32 [8, 8], replicated, may hold values from -2 to 2
- eigen_wave_celerity: float32 [8], replicated, may hold values from 1e-06 to 0.001
- thermal_response_matrix: float32 [8, 8], replicated, may hold values from -2 to 2
Outputs:
- grid_out: bfloat16 [16, 8, 160, 2560], P('groups', None, 'lat'), parts along dimension 0
The draws below stay inside these ranges and needn't reach their ends.
There are 2 independent parts, one for each index of `groups`. The reference program is written for one: setup_inputs(seed, part) draws one part's arguments, and reference() takes and returns one part's arrays. A program takes and returns all parts, laid end to end along the dimension named above; an argument that names none is the same for every part. Nothing has to cross between parts.
Inputs may be any that keep to these rules, and one draw needn't show every extreme that they name: `azimuthal_number_list`: every wavenumber 0 to 639 is held by exactly one slot. `parallel_arrangement`: every latitude 0 to 159 appears at exactly one grid row.
All inputs are finite; a program needn't handle non-finite values.
Results may differ from the reference program's by a relative error of at most 0.0062.
Values may be sent and summed in bfloat16 or wider, within the bound.
No kernel may reach another device: no remote copies, remote signals or barrier semaphores. Data moves between devices by JAX's collectives and lax.ppermute only.
A program may use at most 64 MiB of HBM per device.

```python
import math
import jax
import jax.numpy as jnp
from jax import lax

WAVES = 640
NLON = 2560
FIELDS = 8
LAYER_TOTAL = 8
NLAT = 160


def level_of(rng, dims, shards, least, high):
    def one(axis_at, shards_of):
        steps = jax.random.uniform(jax.random.fold_in(jax.random.fold_in(rng, 6), axis_at), (shards_of,), jnp.float32, least / len(shards), high / len(shards))
        return jnp.repeat(jnp.exp(steps), dims[axis_at] // shards_of).reshape((-1,) + (1,) * (len(dims) - axis_at - 1))

    level = one(*shards[0])
    for cut in shards[1:]:
        level = level * one(*cut)
    return level


def noise(key, dims, scale, reach, pieces=(), kind=jnp.bfloat16):
    gain = level_of(key, dims, pieces, -0.22, 0.18) if pieces else 1.0
    array = jax.random.normal(key, dims, jnp.float32) * scale * gain
    return jnp.minimum(jnp.maximum(array, -reach), reach).astype(kind)


def setup_inputs(seed: int = 0, part: int = 0) -> dict:
    key_list = jax.random.split(jax.random.key(seed), 9)
    part_splits = jax.random.split(jax.random.fold_in(key_list[8], part), 9)
    return {
        "harmonic_right_sides": noise(part_splits[0], (FIELDS, LAYER_TOTAL, 2, WAVES, WAVES), (WAVES ** -0.5), 0.625, ((3, 16),), jnp.float32),
        "azimuthal_number_list": jax.random.permutation(key_list[1], WAVES).astype(jnp.int32),
        "parallel_arrangement": jax.random.permutation(key_list[2], NLAT).astype(jnp.int32),
        "polar_basis_values": noise(key_list[3], (WAVES, NLAT, WAVES), WAVES ** -0.5, 0.25, ((0, 16),)),
        "eigen_forward_matrix": noise(key_list[4], (LAYER_TOTAL, LAYER_TOTAL), LAYER_TOTAL ** -0.5, 2.0, (), jnp.float32),
        "eigen_back_matrix": noise(key_list[5], (LAYER_TOTAL, LAYER_TOTAL), LAYER_TOTAL ** -0.5, 2.0, (), jnp.float32),
        "eigen_wave_celerity": jnp.clip(jnp.exp(jax.random.uniform(key_list[6], (LAYER_TOTAL,), jnp.float32, math.log(9.999999974752427e-07), math.log(0.001))), 9.999999974752427e-07, 0.001),
        "thermal_response_matrix": noise(key_list[7], (LAYER_TOTAL, LAYER_TOTAL), LAYER_TOTAL ** -0.5, 2.0, (), jnp.float32),
    }


full_circle_radians = 6.283185307179586


def wave_table(azimuthal_number_list, nlon):
    longitude = jnp.arange(nlon, dtype=jnp.int32)
    coupled_product = (azimuthal_number_list.astype(jnp.int32)[:, None] * longitude[None, :]) % nlon
    phase_angle = coupled_product.astype(jnp.float32) * (full_circle_radians / nlon)
    weight = jnp.where(azimuthal_number_list == 0, 1.0, 2.0).astype(jnp.float32)[:, None]
    return jnp.stack([weight * jnp.cos(phase_angle), -weight * jnp.sin(phase_angle)], 0).astype(jnp.bfloat16)


def implicit_update_quantities(harmonic_right_sides, position_labels, eigen_forward_matrix, eigen_back_matrix, eigen_wave_celerity, thermal_response_matrix):
    offsets = jnp.arange(harmonic_right_sides.shape[-1], dtype=jnp.int32)
    total_n = position_labels.astype(jnp.int32)[:, None] + offsets[None, :]
    inside = total_n < harmonic_right_sides.shape[-1]
    degree = total_n.astype(jnp.float32)
    laplace_eigen = degree * (degree + 1.0)
    maximal_order = lax.Precision.HIGHEST
    modal_part = jnp.einsum("ml,lcsk->mcsk", eigen_forward_matrix, harmonic_right_sides[0], precision=maximal_order)
    damped = modal_part / (1.0 + eigen_wave_celerity[:, None, None, None] * laplace_eigen)
    spreading_rate_plane = jnp.einsum("kp,phli->khli", eigen_back_matrix, damped, precision=maximal_order)
    thermal_quantity = harmonic_right_sides[1] - jnp.einsum("kp,phli->khli", thermal_response_matrix, spreading_rate_plane, precision=maximal_order)
    quantity_pile = jnp.concatenate([spreading_rate_plane[None], thermal_quantity[None], harmonic_right_sides[2:]], 0)
    return jnp.where(inside, quantity_pile, jnp.zeros_like(quantity_pile)).astype(jnp.bfloat16)


def reference(harmonic_right_sides, azimuthal_number_list, parallel_arrangement, polar_basis_values, eigen_forward_matrix, eigen_back_matrix, eigen_wave_celerity, thermal_response_matrix):
    harmonic_weights = implicit_update_quantities(harmonic_right_sides, azimuthal_number_list, eigen_forward_matrix, eigen_back_matrix, eigen_wave_celerity, thermal_response_matrix)
    row_count = FIELDS * LAYER_TOTAL
    by_slot = jnp.moveaxis(harmonic_weights.reshape(row_count * 2, WAVES, WAVES), 1, 0)

    def one_slot(paired):
        block, plane = paired
        return jnp.dot(block.astype(jnp.float32), plane.astype(jnp.float32).T, preferred_element_type=jnp.float32)

    natural = lax.map(one_slot, (by_slot, polar_basis_values))
    fourier = jnp.take(natural, parallel_arrangement, axis=2).astype(jnp.bfloat16)
    fourier = fourier.reshape(WAVES, row_count, 2, NLAT)
    fourier = jnp.transpose(fourier, (1, 3, 2, 0)).reshape(FIELDS, LAYER_TOTAL * NLAT, 2 * WAVES)
    table = wave_table(azimuthal_number_list, NLON).reshape(2 * WAVES, NLON).astype(jnp.float32)

    def one_field(block):
        return jnp.dot(block.astype(jnp.float32), table, preferred_element_type=jnp.float32).astype(jnp.bfloat16)

    grid_out = lax.map(one_field, fourier)
    return grid_out.reshape(FIELDS, LAYER_TOTAL, NLAT, NLON)
```

```python
import functools
import jax
import jax.numpy as jnp
from jax import lax
from jax.experimental import pallas as pl
from jax.experimental.pallas import tpu as pltpu
from jax.sharding import PartitionSpec as P

NLON = 2560
LANES = 128
SUBLANES = 8
full_circle_radians = 6.283185307179586


def wave_table(azimuthal_number_list, nlon):
    longitude = jnp.arange(nlon, dtype=jnp.int32)
    coupled_product = azimuthal_number_list[:, None] * longitude[None, :] % nlon
    phase_angle = coupled_product.astype(jnp.float32) * (full_circle_radians / nlon)
    weight = jnp.where(azimuthal_number_list == 0, 1.0, 2.0).astype(jnp.float32)[:, None]
    return jnp.stack([weight * jnp.cos(phase_angle), -weight * jnp.sin(phase_angle)], 0).astype(
        jnp.bfloat16
    )


def implicit_update_quantities(rhs, position_labels, forward, back, celerity, thermal):
    offsets = jnp.arange(rhs.shape[-1], dtype=jnp.int32)
    total_n = position_labels[:, None] + offsets[None, :]
    inside = total_n < rhs.shape[-1]
    degree = total_n.astype(jnp.float32)
    laplace_eigen = degree * (degree + 1.0)
    high = lax.Precision.HIGHEST
    modal_part = jnp.einsum("ml,lcsk->mcsk", forward, rhs[0], precision=high)
    damped = modal_part / (1.0 + celerity[:, None, None, None] * laplace_eigen)
    divergence = jnp.einsum("kp,phli->khli", back, damped, precision=high)
    temperature = rhs[1] - jnp.einsum("kp,phli->khli", thermal, divergence, precision=high)
    pile = jnp.concatenate([divergence[None], temperature[None], rhs[2:]], 0)
    return jnp.where(inside, pile, jnp.zeros_like(pile)).astype(jnp.bfloat16)


def per_device_plain(rhs, azimuthal, arrangement, polar, forward, back, celerity, thermal):
    fields, levels = rhs.shape[:2]
    slots, nlat, waves = polar.shape
    lat_dev = nlat // lax.axis_size("lat")
    labels = lax.dynamic_slice_in_dim(azimuthal, lax.axis_index("lat") * slots, slots)
    coeffs = implicit_update_quantities(rhs, labels, forward, back, celerity, thermal)
    rows = fields * levels
    natural = jnp.einsum(
        "rsk,slk->rsl",
        coeffs.reshape(rows * 2, slots, waves),
        polar,
        preferred_element_type=jnp.float32,
    )
    fourier = jnp.take(natural, arrangement, axis=2).astype(jnp.bfloat16)
    fourier = fourier.reshape(rows, 2, slots, nlat)
    grid_out = jnp.einsum(
        "icsr,csj->irj",
        lax.all_to_all(fourier, "lat", split_axis=3, concat_axis=2, tiled=True),
        wave_table(azimuthal, NLON),
        preferred_element_type=jnp.float32,
    ).astype(jnp.bfloat16)
    return grid_out.reshape(fields, levels, lat_dev, NLON)


def legendre_kernel(
    azim_ref, arr_ref, fwd_ref, back_ref, cel_ref, therm_ref, *refs, levels, slots, nlat, waves
):
    tiles = waves // LANES
    rhs_refs = refs[:tiles]
    polar_ref, out_ref, nat_ref, upd_ref = refs[tiles:]
    rows = rhs_refs[0].shape[0]
    step = pl.program_id(0)
    first = lax.axis_index("lat") * slots + step * SUBLANES

    sub = lax.broadcasted_iota(jnp.int32, (SUBLANES, LANES), 0)
    lane = lax.broadcasted_iota(jnp.int32, (SUBLANES, LANES), 1)
    label = jnp.zeros((SUBLANES, LANES), jnp.int32)
    for s in range(SUBLANES):
        label = jnp.where(sub == s, azim_ref[first + s], label)

    for t in range(tiles):
        degree = (label + lane + t * LANES).astype(jnp.float32)
        laplace = degree * (degree + 1.0)
        den = [1.0 / (1.0 + cel_ref[m] * laplace) for m in range(levels)]
        ref = rhs_refs[t]
        x0 = [[ref[l * 2 + c] for c in range(2)] for l in range(levels)]
        damped = []
        for m in range(levels):
            acc = [fwd_ref[m, 0] * x0[0][c] for c in range(2)]
            for l in range(1, levels):
                acc = [acc[c] + fwd_ref[m, l] * x0[l][c] for c in range(2)]
            damped.append([acc[c] * den[m] for c in range(2)])
        div = []
        for l in range(levels):
            acc = [back_ref[l, 0] * damped[0][c] for c in range(2)]
            for m in range(1, levels):
                acc = [acc[c] + back_ref[l, m] * damped[m][c] for c in range(2)]
            div.append(acc)
            for c in range(2):
                upd_ref[t, pl.ds((l * 2 + c) * SUBLANES, SUBLANES), :] = acc[c]
        for l in range(levels):
            acc = [therm_ref[l, 0] * div[0][c] for c in range(2)]
            for q in range(1, levels):
                acc = [acc[c] + therm_ref[l, q] * div[q][c] for c in range(2)]
            for c in range(2):
                upd_ref[t, pl.ds(((levels + l) * 2 + c) * SUBLANES, SUBLANES), :] = (
                    ref[(levels + l) * 2 + c] - acc[c]
                )

    solved = 4 * levels
    rest = rows - solved
    for s in range(SUBLANES):
        room = waves - azim_ref[first + s]
        pieces = []
        for t in range(tiles):
            flat = rhs_refs[t].reshape(rows * SUBLANES, LANES)
            parts = []
            for c in range(2):
                parts.append(
                    upd_ref[t, pl.ds(c * SUBLANES + s, solved // 2, stride=2 * SUBLANES), :]
                )
                parts.append(
                    flat[pl.ds((solved + c) * SUBLANES + s, rest // 2, stride=2 * SUBLANES), :]
                )
            piece = jnp.concatenate(parts, 0)
            k = lax.broadcasted_iota(jnp.int32, piece.shape, 1) + t * LANES
            pieces.append(jnp.where(k < room, piece, 0.0).astype(jnp.bfloat16))
        coeffs = jnp.concatenate(pieces, 1)
        product = lax.dot_general(
            polar_ref[s], coeffs, (((1,), (1,)), ((), ())), preferred_element_type=jnp.float32
        )
        nat_ref[pl.ds((step * SUBLANES + s) * nlat, nlat), :] = product

    @pl.when(step == pl.num_programs(0) - 1)
    def _():
        half = LANES // 2
        low = lax.broadcasted_iota(jnp.int32, (slots, LANES), 1) < half

        def pair(p, carry):
            a = nat_ref[pl.ds(arr_ref[2 * p], slots, stride=nlat), :]
            b = nat_ref[pl.ds(arr_ref[2 * p + 1], slots, stride=nlat), :]
            real = jnp.where(low, a, pltpu.roll(b, half, 1))
            imag = jnp.where(low, pltpu.roll(a, half, 1), b)
            out_ref[p] = jnp.concatenate([real, imag], 0).astype(jnp.bfloat16)
            return carry

        lax.fori_loop(0, nlat // 2, pair, 0, unroll=4)


def legendre(rhs, azimuthal, arrangement, polar, forward, back, celerity, thermal):
    fields, levels = rhs.shape[:2]
    slots, nlat, waves = polar.shape
    rows = fields * levels * 2
    tiles = waves // LANES
    smem = pl.BlockSpec(memory_space=pltpu.SMEM)
    flat = rhs.reshape(rows, slots, waves)
    rhs_specs = [
        pl.BlockSpec((rows, SUBLANES, LANES), functools.partial(lambda t, i: (0, i, t), t))
        for t in range(tiles)
    ]
    return pl.pallas_call(
        functools.partial(
            legendre_kernel, levels=levels, slots=slots, nlat=nlat, waves=waves
        ),
        grid=(slots // SUBLANES,),
        in_specs=[smem] * 6
        + rhs_specs
        + [pl.BlockSpec((SUBLANES, nlat, waves), lambda i: (i, 0, 0))],
        out_specs=pl.BlockSpec((nlat // 2, 2 * slots, LANES), lambda i: (0, 0, 0)),
        out_shape=jax.ShapeDtypeStruct((nlat // 2, 2 * slots, LANES), jnp.bfloat16),
        scratch_shapes=[
            pltpu.VMEM((slots * nlat, LANES), jnp.float32),
            pltpu.VMEM((tiles, 4 * levels * SUBLANES, LANES), jnp.float32),
        ],
        compiler_params=pltpu.CompilerParams(vmem_limit_bytes=36 * 1024 * 1024),
        name="legendre",
    )(azimuthal, arrangement, forward, back, celerity, thermal, *([flat] * tiles), polar)


def table_kernel(azim_ref, out_ref, *, slots, nlon):
    blocks = nlon // LANES
    m = azim_ref[0]
    lane = lax.broadcasted_iota(jnp.int32, (slots, LANES), 1)
    unit = full_circle_radians / nlon
    fine = ((m * lane) % nlon).astype(jnp.float32) * unit
    coarse = ((m * lane) % blocks).astype(jnp.float32) * (unit * LANES)
    weight = jnp.where(m == 0, 1.0, 2.0)
    cos_fine = weight * jnp.cos(fine)
    sin_fine = weight * jnp.sin(fine)
    cos_coarse = jnp.cos(coarse)
    sin_coarse = jnp.sin(coarse)
    for b in range(blocks):
        cc = cos_coarse[:, b : b + 1]
        sc = sin_coarse[:, b : b + 1]
        real = cos_fine * cc - sin_fine * sc
        imag = -(sin_fine * cc + cos_fine * sc)
        out_ref[0, :, b * LANES : (b + 1) * LANES] = jnp.concatenate([real, imag], 0).astype(
            jnp.bfloat16
        )


def table(azimuthal, devices, slots):
    spread = jnp.broadcast_to(azimuthal.reshape(devices, slots, 1), (devices, slots, LANES))
    return pl.pallas_call(
        functools.partial(table_kernel, slots=slots, nlon=NLON),
        grid=(devices,),
        in_specs=[pl.BlockSpec((1, slots, LANES), lambda d: (d, 0, 0))],
        out_specs=pl.BlockSpec((1, 2 * slots, NLON), lambda d: (d, 0, 0)),
        out_shape=jax.ShapeDtypeStruct((devices, 2 * slots, NLON), jnp.bfloat16),
        compiler_params=pltpu.CompilerParams(vmem_limit_bytes=16 * 1024 * 1024),
        name="table",
    )(spread)


def grid_kernel(x_ref, tab_ref, out_ref, lhs_ref, acc_ref, *, lat_dev):
    depth = tab_ref.shape[0]
    tiles = tab_ref.shape[1] // LANES
    half = LANES // 2

    @pl.when(pl.program_id(0) == 0)
    def _():
        for p in range(lat_dev // 2):
            block = x_ref[:, p].reshape(depth, LANES)
            lhs_ref[pl.ds(p * LANES, LANES), :] = block.T

    product = jnp.dot(lhs_ref[...], tab_ref[...], preferred_element_type=jnp.float32)
    for t in range(tiles):
        acc_ref[t] = product[:, t * LANES : (t + 1) * LANES]

    for t in range(tiles):
        for i in range(half):
            out_ref[i, :, t * LANES : (t + 1) * LANES] = acc_ref[
                t, pl.ds(i, lat_dev, stride=half), :
            ].astype(jnp.bfloat16)


def grid_product(received, tab, lat_dev, block=512):
    devices = received.shape[0]
    depth = tab.shape[0] * tab.shape[1]
    half = LANES // 2
    x = received.reshape(devices, lat_dev // 2, depth // devices, LANES)
    return pl.pallas_call(
        functools.partial(grid_kernel, lat_dev=lat_dev),
        grid=(NLON // block,),
        in_specs=[
            pl.BlockSpec(x.shape, lambda j: (0, 0, 0, 0)),
            pl.BlockSpec((depth, block), lambda j: (0, j)),
        ],
        out_specs=pl.BlockSpec((half, lat_dev, block), lambda j: (0, 0, j)),
        out_shape=jax.ShapeDtypeStruct((half, lat_dev, NLON), jnp.bfloat16),
        scratch_shapes=[
            pltpu.VMEM((lat_dev * half, depth), jnp.bfloat16),
            pltpu.VMEM((block // LANES, lat_dev * half, LANES), jnp.float32),
        ],
        compiler_params=pltpu.CompilerParams(vmem_limit_bytes=24 * 1024 * 1024),
        name="grid_product",
    )(x, tab.reshape(depth, NLON))


def per_device(rhs, azimuthal, arrangement, polar, forward, back, celerity, thermal):
    fields, levels = rhs.shape[:2]
    slots, nlat, waves = polar.shape
    devices = lax.axis_size("lat")
    lat_dev = nlat // devices
    packed = legendre(rhs, azimuthal, arrangement, polar, forward, back, celerity, thermal)
    packed = packed.reshape(devices, lat_dev * slots, LANES)
    received = lax.all_to_all(packed, "lat", split_axis=0, concat_axis=0, tiled=True)
    tab = table(azimuthal, devices, slots)
    grid_out = grid_product(received, tab, lat_dev)
    return grid_out.reshape(fields, levels, lat_dev, NLON)


def solution(mesh):
    in_specs = (
        P("groups", None, None, "lat", None),
        P(),
        P(),
        P("lat", None, None),
        P(),
        P(),
        P(),
        P(),
    )
    out_specs = P("groups", None, "lat", None)

    def body(rhs, azimuthal, arrangement, polar, *matrices):
        slots, nlat, waves = polar.shape
        lat_dev = nlat // lax.axis_size("lat")
        fits = (
            slots % SUBLANES == 0
            and waves % LANES == 0
            and lat_dev % 2 == 0
            and 2 * rhs.shape[0] * rhs.shape[1] == LANES
            and rhs.shape[0] > 2
        )
        form = per_device if fits else per_device_plain
        return form(rhs, azimuthal, arrangement, polar, *matrices)

    return jax.shard_map(
        body, mesh=mesh, in_specs=in_specs, out_specs=out_specs, check_vma=False
    )
```

```python
import functools
import jax
import jax.numpy as jnp
from jax import lax
from jax.experimental import pallas as pl
from jax.experimental.pallas import tpu as pltpu
from jax.sharding import PartitionSpec as P

NLON = 2560
LANES = 128
SUBLANES = 8
full_circle_radians = 6.283185307179586


def wave_table(azimuthal_number_list, nlon):
    longitude = jnp.arange(nlon, dtype=jnp.int32)
    coupled_product = azimuthal_number_list[:, None] * longitude[None, :] % nlon
    phase_angle = coupled_product.astype(jnp.float32) * (full_circle_radians / nlon)
    weight = jnp.where(azimuthal_number_list == 0, 1.0, 2.0).astype(jnp.float32)[:, None]
    return jnp.stack([weight * jnp.cos(phase_angle), -weight * jnp.sin(phase_angle)], 0).astype(
        jnp.bfloat16
    )


def implicit_update_quantities(rhs, position_labels, forward, back, celerity, thermal):
    offsets = jnp.arange(rhs.shape[-1], dtype=jnp.int32)
    total_n = position_labels[:, None] + offsets[None, :]
    inside = total_n < rhs.shape[-1]
    degree = total_n.astype(jnp.float32)
    laplace_eigen = degree * (degree + 1.0)
    high = lax.Precision.HIGHEST
    modal_part = jnp.einsum("ml,lcsk->mcsk", forward, rhs[0], precision=high)
    damped = modal_part / (1.0 + celerity[:, None, None, None] * laplace_eigen)
    divergence = jnp.einsum("kp,phli->khli", back, damped, precision=high)
    temperature = rhs[1] - jnp.einsum("kp,phli->khli", thermal, divergence, precision=high)
    pile = jnp.concatenate([divergence[None], temperature[None], rhs[2:]], 0)
    return jnp.where(inside, pile, jnp.zeros_like(pile)).astype(jnp.bfloat16)


def per_device_plain(rhs, azimuthal, arrangement, polar, forward, back, celerity, thermal):
    fields, levels = rhs.shape[:2]
    slots, nlat, waves = polar.shape
    lat_dev = nlat // lax.axis_size("lat")
    labels = lax.dynamic_slice_in_dim(azimuthal, lax.axis_index("lat") * slots, slots)
    coeffs = implicit_update_quantities(rhs, labels, forward, back, celerity, thermal)
    rows = fields * levels
    natural = jnp.einsum(
        "rsk,slk->rsl",
        coeffs.reshape(rows * 2, slots, waves),
        polar,
        preferred_element_type=jnp.float32,
    )
    fourier = jnp.take(natural, arrangement, axis=2).astype(jnp.bfloat16)
    fourier = fourier.reshape(rows, 2, slots, nlat)
    grid_out = jnp.einsum(
        "icsr,csj->irj",
        lax.all_to_all(fourier, "lat", split_axis=3, concat_axis=2, tiled=True),
        wave_table(azimuthal, NLON),
        preferred_element_type=jnp.float32,
    ).astype(jnp.bfloat16)
    return grid_out.reshape(fields, levels, lat_dev, NLON)


def legendre_kernel(
    azim_hbm, arr_hbm, fwd_hbm, back_hbm, cel_hbm, therm_hbm, *refs, levels, slots, nlat, waves
):
    tiles = waves // LANES
    rhs_refs = refs[:tiles]
    polar_ref, out_ref, nat_ref, pad_ref = refs[tiles : tiles + 4]
    scalars, sems = refs[tiles + 4 : -1], refs[-1]
    azim_ref, arr_ref, fwd_ref, back_ref, cel_ref, therm_ref = scalars
    sources = (azim_hbm, arr_hbm, fwd_hbm, back_hbm, cel_hbm, therm_hbm)
    copies = [
        pltpu.make_async_copy(src, dst, sems.at[i])
        for i, (src, dst) in enumerate(zip(sources, scalars))
    ]
    rows = rhs_refs[0].shape[0]
    pitch = row_pitch()
    apart = slot_pitch(nlat)
    step = pl.program_id(0)

    @pl.when(step == 0)
    def _():
        for copy in copies:
            copy.start()
        for copy in copies:
            copy.wait()

    first = lax.axis_index("lat") * slots + step * SUBLANES
    sub = lax.broadcasted_iota(jnp.int32, (SUBLANES, LANES), 0)
    lane = lax.broadcasted_iota(jnp.int32, (SUBLANES, LANES), 1)
    label = jnp.zeros((SUBLANES, LANES), jnp.int32)
    for s in range(SUBLANES):
        label = jnp.where(sub == s, azim_ref[first + s], label)

    for group in range(0, tiles, 2):
        ts = list(range(group, min(group + 2, tiles)))
        parts = [(t, c) for t in ts for c in range(2)]
        span = range(len(parts))

        def mix(matrix, row, operand):
            acc = [matrix[row, 0] * operand[0][i] for i in span]
            for q in range(1, levels):
                acc = [acc[i] + matrix[row, q] * operand[q][i] for i in span]
            return acc

        laplace = []
        for t in ts:
            degree = (label + lane + t * LANES).astype(jnp.float32)
            laplace.append(degree * (degree + 1.0))
        x0 = [[rhs_refs[t][l * 2 + c] for t, c in parts] for l in range(levels)]
        damped = []
        for m in range(levels):
            modal = mix(fwd_ref, m, x0)
            den = [1.0 / (1.0 + cel_ref[m] * lap) for lap in laplace]
            damped.append([modal[i] * den[i // 2] for i in span])
        div = []
        for l in range(levels):
            div.append(mix(back_ref, l, damped))
            for i, (t, c) in enumerate(parts):
                pad_ref[t, pl.ds((l * 2 + c) * pitch, SUBLANES), :] = div[l][i]
        for l in range(levels):
            response = mix(therm_ref, l, div)
            for i, (t, c) in enumerate(parts):
                row = (levels + l) * 2 + c
                pad_ref[t, pl.ds(row * pitch, SUBLANES), :] = rhs_refs[t][row] - response[i]

    for t in range(tiles):
        for row in range(4 * levels, rows):
            pad_ref[t, pl.ds(row * pitch, SUBLANES), :] = rhs_refs[t][row]

    for s in range(SUBLANES):
        room = waves - azim_ref[first + s]
        pieces = []
        for t in range(tiles):
            piece = jnp.concatenate(
                [pad_ref[t, pl.ds(c * pitch + s, rows // 2, stride=2 * pitch), :] for c in range(2)],
                0,
            )
            k = lax.broadcasted_iota(jnp.int32, piece.shape, 1) + t * LANES
            pieces.append(jnp.where(k < room, piece, 0.0).astype(jnp.bfloat16))
        coeffs = jnp.concatenate(pieces, 1)
        product = lax.dot_general(
            polar_ref[s], coeffs, (((1,), (1,)), ((), ())), preferred_element_type=jnp.float32
        )
        nat_ref[pl.ds((step * SUBLANES + s) * apart, nlat), :] = product

    @pl.when(step == pl.num_programs(0) - 1)
    def _():
        half = LANES // 2
        low = lax.broadcasted_iota(jnp.int32, (slots, LANES), 1) < half

        def pair(p, carry):
            a = nat_ref[pl.ds(arr_ref[2 * p], slots, stride=apart), :]
            b = nat_ref[pl.ds(arr_ref[2 * p + 1], slots, stride=apart), :]
            real = jnp.where(low, a, pltpu.roll(b, half, 1))
            imag = jnp.where(low, pltpu.roll(a, half, 1), b)
            out_ref[p] = jnp.concatenate([real, imag], 0).astype(jnp.bfloat16)
            return carry

        lax.fori_loop(0, nlat // 2, pair, 0, unroll=4)


def row_pitch():
    return SUBLANES + 1


def slot_pitch(nlat):
    return nlat + 4


def legendre(rhs, azimuthal, arrangement, polar, forward, back, celerity, thermal):
    fields, levels = rhs.shape[:2]
    slots, nlat, waves = polar.shape
    rows = fields * levels * 2
    tiles = waves // LANES
    scalars = (azimuthal, arrangement, forward, back, celerity, thermal)
    flat = rhs.reshape(rows, slots, waves)
    rhs_specs = [
        pl.BlockSpec((rows, SUBLANES, LANES), functools.partial(lambda t, i: (0, i, t), t))
        for t in range(tiles)
    ]
    return pl.pallas_call(
        functools.partial(
            legendre_kernel, levels=levels, slots=slots, nlat=nlat, waves=waves
        ),
        grid=(slots // SUBLANES,),
        in_specs=[pl.BlockSpec(memory_space=pltpu.HBM)] * len(scalars)
        + rhs_specs
        + [pl.BlockSpec((SUBLANES, nlat, waves), lambda i: (i, 0, 0))],
        out_specs=pl.BlockSpec((nlat // 2, 2 * slots, LANES), lambda i: (0, 0, 0)),
        out_shape=jax.ShapeDtypeStruct((nlat // 2, 2 * slots, LANES), jnp.bfloat16),
        scratch_shapes=[
            pltpu.VMEM((slots * slot_pitch(nlat), LANES), jnp.float32),
            pltpu.VMEM((tiles, rows * row_pitch(), LANES), jnp.float32),
        ]
        + [pltpu.SMEM(a.shape, a.dtype) for a in scalars]
        + [pltpu.SemaphoreType.DMA((len(scalars),))],
        compiler_params=pltpu.CompilerParams(vmem_limit_bytes=56 * 1024 * 1024),
        name="legendre",
    )(*scalars, *([flat] * tiles), polar)


def table_kernel(azim_ref, out_ref, *, slots, nlon):
    blocks = nlon // LANES
    m = azim_ref[0]
    lane = lax.broadcasted_iota(jnp.int32, (slots, LANES), 1)
    unit = full_circle_radians / nlon
    fine = ((m * lane) % nlon).astype(jnp.float32) * unit
    coarse = ((m * lane) % blocks).astype(jnp.float32) * (unit * LANES)
    weight = jnp.where(m == 0, 1.0, 2.0)
    cos_fine = weight * jnp.cos(fine)
    sin_fine = weight * jnp.sin(fine)
    cos_coarse = jnp.cos(coarse)
    sin_coarse = jnp.sin(coarse)
    for b in range(blocks):
        cc = cos_coarse[:, b : b + 1]
        sc = sin_coarse[:, b : b + 1]
        real = cos_fine * cc - sin_fine * sc
        imag = -(sin_fine * cc + cos_fine * sc)
        out_ref[0, :, b * LANES : (b + 1) * LANES] = jnp.concatenate([real, imag], 0).astype(
            jnp.bfloat16
        )


def table(azimuthal, devices, slots):
    spread = jnp.broadcast_to(azimuthal.reshape(devices, slots, 1), (devices, slots, LANES))
    return pl.pallas_call(
        functools.partial(table_kernel, slots=slots, nlon=NLON),
        grid=(devices,),
        in_specs=[pl.BlockSpec((1, slots, LANES), lambda d: (d, 0, 0))],
        out_specs=pl.BlockSpec((1, 2 * slots, NLON), lambda d: (d, 0, 0)),
        out_shape=jax.ShapeDtypeStruct((devices, 2 * slots, NLON), jnp.bfloat16),
        compiler_params=pltpu.CompilerParams(vmem_limit_bytes=16 * 1024 * 1024),
        name="table",
    )(spread)


def grid_kernel(x_ref, tab_ref, out_ref, lhs_ref, *, fields, lat_dev):
    depth = tab_ref.shape[0]

    @pl.when(pl.program_id(0) == 0)
    def _():
        for p in range(lat_dev // 2):
            block = x_ref[:, p].reshape(depth, LANES)
            lhs_ref[pl.ds(p * LANES, LANES), :] = block.T

    half = LANES // 2
    levels = half // fields
    product = jnp.dot(lhs_ref[...], tab_ref[...], preferred_element_type=jnp.float32)
    for r in range(lat_dev):
        for f in range(fields):
            row = r * half + f * levels
            out_ref[f, r] = product[row : row + levels].astype(jnp.bfloat16)


def grid_product(received, tab, lat_dev, fields, block=512):
    devices = received.shape[0]
    depth = tab.shape[0] * tab.shape[1]
    half = LANES // 2
    levels = half // fields
    x = received.reshape(devices, lat_dev // 2, depth // devices, LANES)
    out = pl.pallas_call(
        functools.partial(grid_kernel, fields=fields, lat_dev=lat_dev),
        grid=(NLON // block,),
        in_specs=[
            pl.BlockSpec(x.shape, lambda j: (0, 0, 0, 0)),
            pl.BlockSpec((depth, block), lambda j: (0, j)),
        ],
        out_specs=pl.BlockSpec((fields, lat_dev, levels, block), lambda j: (0, 0, 0, j)),
        out_shape=jax.ShapeDtypeStruct((fields, lat_dev, levels, NLON), jnp.bfloat16),
        scratch_shapes=[pltpu.VMEM((lat_dev * half, depth), jnp.bfloat16)],
        compiler_params=pltpu.CompilerParams(vmem_limit_bytes=48 * 1024 * 1024),
        name="grid_product",
    )(x, tab.reshape(depth, NLON))
    return jnp.swapaxes(out, 1, 2)


def per_device(rhs, azimuthal, arrangement, polar, forward, back, celerity, thermal):
    fields, levels = rhs.shape[:2]
    slots, nlat, waves = polar.shape
    devices = lax.axis_size("lat")
    lat_dev = nlat // devices
    packed = legendre(rhs, azimuthal, arrangement, polar, forward, back, celerity, thermal)
    packed = packed.reshape(devices, lat_dev * slots, LANES)
    received = lax.all_to_all(packed, "lat", split_axis=0, concat_axis=0, tiled=True)
    tab = table(azimuthal, devices, slots)
    return grid_product(received, tab, lat_dev, fields)


def solution(mesh):
    in_specs = (
        P("groups", None, None, "lat", None),
        P(),
        P(),
        P("lat", None, None),
        P(),
        P(),
        P(),
        P(),
    )
    out_specs = P("groups", None, "lat", None)

    def body(rhs, azimuthal, arrangement, polar, *matrices):
        slots, nlat, waves = polar.shape
        lat_dev = nlat // lax.axis_size("lat")
        fits = (
            slots % SUBLANES == 0
            and waves % LANES == 0
            and lat_dev % 2 == 0
            and 2 * rhs.shape[0] * rhs.shape[1] == LANES
            and rhs.shape[0] > 2
        )
        form = per_device if fits else per_device_plain
        return form(rhs, azimuthal, arrangement, polar, *matrices)

    return jax.shard_map(
        body, mesh=mesh, in_specs=in_specs, out_specs=out_specs, check_vma=False
    )
```

```python
import functools
import jax
import jax.numpy as jnp
from jax import lax
from jax.experimental import pallas as pl
from jax.experimental.pallas import tpu as pltpu
from jax.sharding import PartitionSpec as P

NLON = 2560
LANES = 128
SUBLANES = 8
GROUP = 2
full_circle_radians = 6.283185307179586


def wave_table(azimuthal_number_list, nlon):
    longitude = jnp.arange(nlon, dtype=jnp.int32)
    coupled_product = azimuthal_number_list[:, None] * longitude[None, :] % nlon
    phase_angle = coupled_product.astype(jnp.float32) * (full_circle_radians / nlon)
    weight = jnp.where(azimuthal_number_list == 0, 1.0, 2.0).astype(jnp.float32)[:, None]
    return jnp.stack([weight * jnp.cos(phase_angle), -weight * jnp.sin(phase_angle)], 0).astype(
        jnp.bfloat16
    )


def implicit_update_quantities(rhs, position_labels, forward, back, celerity, thermal):
    offsets = jnp.arange(rhs.shape[-1], dtype=jnp.int32)
    total_n = position_labels[:, None] + offsets[None, :]
    inside = total_n < rhs.shape[-1]
    degree = total_n.astype(jnp.float32)
    laplace_eigen = degree * (degree + 1.0)
    high = lax.Precision.HIGHEST
    modal_part = jnp.einsum("ml,lcsk->mcsk", forward, rhs[0], precision=high)
    damped = modal_part / (1.0 + celerity[:, None, None, None] * laplace_eigen)
    divergence = jnp.einsum("kp,phli->khli", back, damped, precision=high)
    temperature = rhs[1] - jnp.einsum("kp,phli->khli", thermal, divergence, precision=high)
    pile = jnp.concatenate([divergence[None], temperature[None], rhs[2:]], 0)
    return jnp.where(inside, pile, jnp.zeros_like(pile)).astype(jnp.bfloat16)


def per_device_plain(rhs, azimuthal, arrangement, polar, forward, back, celerity, thermal):
    fields, levels = rhs.shape[:2]
    slots, nlat, waves = polar.shape
    lat_dev = nlat // lax.axis_size("lat")
    labels = lax.dynamic_slice_in_dim(azimuthal, lax.axis_index("lat") * slots, slots)
    coeffs = implicit_update_quantities(rhs, labels, forward, back, celerity, thermal)
    rows = fields * levels
    natural = jnp.einsum(
        "rsk,slk->rsl",
        coeffs.reshape(rows * 2, slots, waves),
        polar,
        preferred_element_type=jnp.float32,
    )
    fourier = jnp.take(natural, arrangement, axis=2).astype(jnp.bfloat16)
    fourier = fourier.reshape(rows, 2, slots, nlat)
    grid_out = jnp.einsum(
        "icsr,csj->irj",
        lax.all_to_all(fourier, "lat", split_axis=3, concat_axis=2, tiled=True),
        wave_table(azimuthal, NLON),
        preferred_element_type=jnp.float32,
    ).astype(jnp.bfloat16)
    return grid_out.reshape(fields, levels, lat_dev, NLON)


def legendre_kernel(
    azim_ref, arr_ref, fwd_ref, back_ref, cel_ref, therm_ref, rhs_ref, polar_ref, out_ref,
    nat_ref, pad_ref, *, levels, slots, nlat, waves
):
    tiles = waves // LANES
    rows = rhs_ref.shape[0]
    pitch = row_pitch()
    apart = slot_pitch(nlat)
    step = pl.program_id(0)

    def rhs(row, t):
        return rhs_ref[row, :, t * LANES : (t + 1) * LANES]

    first = lax.axis_index("lat") * slots + step * SUBLANES
    sub = lax.broadcasted_iota(jnp.int32, (SUBLANES, LANES), 0)
    lane = lax.broadcasted_iota(jnp.int32, (SUBLANES, LANES), 1)
    label = jnp.zeros((SUBLANES, LANES), jnp.int32)
    for s in range(SUBLANES):
        label = jnp.where(sub == s, azim_ref[first + s], label)

    for group in range(0, tiles, GROUP):
        ts = list(range(group, min(group + GROUP, tiles)))
        parts = [(t, c) for t in ts for c in range(2)]
        span = range(len(parts))

        def mix(matrix, row, operand):
            acc = [matrix[row, 0] * operand[0][i] for i in span]
            for q in range(1, levels):
                acc = [acc[i] + matrix[row, q] * operand[q][i] for i in span]
            return acc

        laplace = []
        for t in ts:
            degree = (label + lane + t * LANES).astype(jnp.float32)
            laplace.append(degree * (degree + 1.0))
        x0 = [[rhs(l * 2 + c, t) for t, c in parts] for l in range(levels)]
        damped = []
        for m in range(levels):
            modal = mix(fwd_ref, m, x0)
            den = [1.0 / (1.0 + cel_ref[m] * lap) for lap in laplace]
            damped.append([modal[i] * den[i // 2] for i in span])
        div = []
        for l in range(levels):
            div.append(mix(back_ref, l, damped))
            for i, (t, c) in enumerate(parts):
                pad_ref[t, pl.ds((l * 2 + c) * pitch, SUBLANES), :] = div[l][i]
        for l in range(levels):
            response = mix(therm_ref, l, div)
            for i, (t, c) in enumerate(parts):
                row = (levels + l) * 2 + c
                pad_ref[t, pl.ds(row * pitch, SUBLANES), :] = rhs(row, t) - response[i]

    for t in range(tiles):
        for row in range(4 * levels, rows):
            pad_ref[t, pl.ds(row * pitch, SUBLANES), :] = rhs(row, t)

    for s in range(SUBLANES):
        room = waves - azim_ref[first + s]
        pieces = []
        for t in range(tiles):
            piece = jnp.concatenate(
                [pad_ref[t, pl.ds(c * pitch + s, rows // 2, stride=2 * pitch), :] for c in range(2)],
                0,
            )
            k = lax.broadcasted_iota(jnp.int32, piece.shape, 1) + t * LANES
            pieces.append(jnp.where(k < room, piece, 0.0).astype(jnp.bfloat16))
        coeffs = jnp.concatenate(pieces, 1)
        product = lax.dot_general(
            polar_ref[s], coeffs, (((1,), (1,)), ((), ())), preferred_element_type=jnp.float32
        )
        nat_ref[pl.ds(s * apart, nlat), :] = product

    half = LANES // 2
    low = lane < half
    pairs = out_ref.shape[1] // (2 * SUBLANES)
    for p in range(nlat // 2):
        a = nat_ref[pl.ds(arr_ref[2 * p], SUBLANES, stride=apart), :]
        b = nat_ref[pl.ds(arr_ref[2 * p + 1], SUBLANES, stride=apart), :]
        real = jnp.where(low, a, pltpu.roll(b, half, 1))
        imag = jnp.where(low, pltpu.roll(a, half, 1), b)
        out_ref[p // pairs, pl.ds(p % pairs * 2 * SUBLANES, 2 * SUBLANES), :] = jnp.concatenate(
            [real, imag], 0
        ).astype(jnp.bfloat16)


def row_pitch():
    return SUBLANES + 1


def slot_pitch(nlat):
    return nlat + 4


def legendre(rhs, azimuthal, arrangement, polar, forward, back, celerity, thermal):
    fields, levels = rhs.shape[:2]
    slots, nlat, waves = polar.shape
    rows = fields * levels * 2
    tiles = waves // LANES
    devices = lax.axis_size("lat")
    steps = slots // SUBLANES
    depth = nlat // devices * SUBLANES
    scalars = (azimuthal, arrangement, forward, back, celerity, thermal)
    return pl.pallas_call(
        functools.partial(
            legendre_kernel, levels=levels, slots=slots, nlat=nlat, waves=waves
        ),
        grid=(steps,),
        in_specs=[pl.BlockSpec(memory_space=pltpu.SMEM)] * len(scalars)
        + [
            pl.BlockSpec((rows, SUBLANES, waves), lambda i: (0, i, 0)),
            pl.BlockSpec((SUBLANES, nlat, waves), lambda i: (i, 0, 0)),
        ],
        out_specs=pl.BlockSpec((devices, None, depth, LANES), lambda i: (0, i, 0, 0)),
        out_shape=jax.ShapeDtypeStruct((devices, steps, depth, LANES), jnp.bfloat16),
        scratch_shapes=[
            pltpu.VMEM((SUBLANES * slot_pitch(nlat), LANES), jnp.float32),
            pltpu.VMEM((tiles, rows * row_pitch(), LANES), jnp.float32),
        ],
        compiler_params=pltpu.CompilerParams(vmem_limit_bytes=60 * 1024 * 1024),
        name="legendre",
    )(*scalars, rhs.reshape(rows, slots, waves), polar)


def table_kernel(azim_ref, out_ref, *, slots, nlon):
    blocks = nlon // LANES
    m = azim_ref[0]
    lane = lax.broadcasted_iota(jnp.int32, (slots, LANES), 1)
    unit = full_circle_radians / nlon
    fine = ((m * lane) % nlon).astype(jnp.float32) * unit
    coarse = ((m * lane) % blocks).astype(jnp.float32) * (unit * LANES)
    weight = jnp.where(m == 0, 1.0, 2.0)
    cos_fine = weight * jnp.cos(fine)
    sin_fine = weight * jnp.sin(fine)
    cos_coarse = jnp.cos(coarse)
    sin_coarse = jnp.sin(coarse)
    for b in range(blocks):
        cc = cos_coarse[:, b : b + 1]
        sc = sin_coarse[:, b : b + 1]
        real = cos_fine * cc - sin_fine * sc
        imag = -(sin_fine * cc + cos_fine * sc)
        rows = []
        for s in range(0, slots, SUBLANES):
            rows += [real[s : s + SUBLANES], imag[s : s + SUBLANES]]
        out_ref[0, :, b * LANES : (b + 1) * LANES] = jnp.concatenate(rows, 0).astype(jnp.bfloat16)


def table(azimuthal, devices, slots):
    spread = jnp.broadcast_to(azimuthal.reshape(devices, slots, 1), (devices, slots, LANES))
    return pl.pallas_call(
        functools.partial(table_kernel, slots=slots, nlon=NLON),
        grid=(devices,),
        in_specs=[pl.BlockSpec((1, slots, LANES), lambda d: (d, 0, 0))],
        out_specs=pl.BlockSpec((1, 2 * slots, NLON), lambda d: (d, 0, 0)),
        out_shape=jax.ShapeDtypeStruct((devices, 2 * slots, NLON), jnp.bfloat16),
        compiler_params=pltpu.CompilerParams(vmem_limit_bytes=16 * 1024 * 1024),
        name="table",
    )(spread)


def grid_kernel(x_ref, tab_ref, out_ref, lhs_ref, *, fields, lat_dev):
    depth = tab_ref.shape[0]

    @pl.when(pl.program_id(0) == 0)
    def _():
        for p in range(lat_dev // 2):
            block = x_ref[:, :, p].reshape(depth, LANES)
            lhs_ref[pl.ds(p * LANES, LANES), :] = block.T

    half = LANES // 2
    levels = half // fields
    product = jnp.dot(lhs_ref[...], tab_ref[...], preferred_element_type=jnp.float32)
    for r in range(lat_dev):
        for f in range(fields):
            row = r * half + f * levels
            out_ref[f, r] = product[row : row + levels].astype(jnp.bfloat16)


def grid_product(received, tab, lat_dev, fields, block=512):
    devices, steps = received.shape[:2]
    depth = tab.shape[0] * tab.shape[1]
    half = LANES // 2
    levels = half // fields
    x = received.reshape(devices, steps, lat_dev // 2, 2 * SUBLANES, LANES)
    out = pl.pallas_call(
        functools.partial(grid_kernel, fields=fields, lat_dev=lat_dev),
        grid=(NLON // block,),
        in_specs=[
            pl.BlockSpec(memory_space=pltpu.VMEM),
            pl.BlockSpec((depth, block), lambda j: (0, j)),
        ],
        out_specs=pl.BlockSpec((fields, lat_dev, levels, block), lambda j: (0, 0, 0, j)),
        out_shape=jax.ShapeDtypeStruct((fields, lat_dev, levels, NLON), jnp.bfloat16),
        scratch_shapes=[pltpu.VMEM((lat_dev * half, depth), jnp.bfloat16)],
        compiler_params=pltpu.CompilerParams(vmem_limit_bytes=48 * 1024 * 1024),
        name="grid_product",
    )(x, tab.reshape(depth, NLON))
    return jnp.swapaxes(out, 1, 2)


def per_device(rhs, azimuthal, arrangement, polar, forward, back, celerity, thermal):
    fields, levels = rhs.shape[:2]
    slots, nlat, waves = polar.shape
    devices = lax.axis_size("lat")
    lat_dev = nlat // devices
    packed = legendre(rhs, azimuthal, arrangement, polar, forward, back, celerity, thermal)
    received = lax.all_to_all(packed, "lat", split_axis=0, concat_axis=0, tiled=True)
    tab = table(azimuthal, devices, slots)
    return grid_product(received, tab, lat_dev, fields)


def solution(mesh):
    in_specs = (
        P("groups", None, None, "lat", None),
        P(),
        P(),
        P("lat", None, None),
        P(),
        P(),
        P(),
        P(),
    )
    out_specs = P("groups", None, "lat", None)

    def body(rhs, azimuthal, arrangement, polar, *matrices):
        slots, nlat, waves = polar.shape
        lat_dev = nlat // lax.axis_size("lat")
        fits = (
            slots % SUBLANES == 0
            and waves % LANES == 0
            and lat_dev % 2 == 0
            and 2 * rhs.shape[0] * rhs.shape[1] == LANES
            and rhs.shape[0] > 2
        )
        form = per_device if fits else per_device_plain
        return form(rhs, azimuthal, arrangement, polar, *matrices)

    return jax.shard_map(
        body, mesh=mesh, in_specs=in_specs, out_specs=out_specs, check_vma=False
    )
```

```python
import functools
import jax
import jax.numpy as jnp
from jax import lax
from jax.experimental import pallas as pl
from jax.experimental.pallas import tpu as pltpu
from jax.sharding import PartitionSpec as P

NLON = 2560
LANES = 128
SUBLANES = 8
GROUP = 2
full_circle_radians = 6.283185307179586


def wave_table(azimuthal_number_list, nlon):
    longitude = jnp.arange(nlon, dtype=jnp.int32)
    coupled_product = azimuthal_number_list[:, None] * longitude[None, :] % nlon
    phase_angle = coupled_product.astype(jnp.float32) * (full_circle_radians / nlon)
    weight = jnp.where(azimuthal_number_list == 0, 1.0, 2.0).astype(jnp.float32)[:, None]
    return jnp.stack([weight * jnp.cos(phase_angle), -weight * jnp.sin(phase_angle)], 0).astype(
        jnp.bfloat16
    )


def implicit_update_quantities(rhs, position_labels, forward, back, celerity, thermal):
    offsets = jnp.arange(rhs.shape[-1], dtype=jnp.int32)
    total_n = position_labels[:, None] + offsets[None, :]
    inside = total_n < rhs.shape[-1]
    degree = total_n.astype(jnp.float32)
    laplace_eigen = degree * (degree + 1.0)
    high = lax.Precision.HIGHEST
    modal_part = jnp.einsum("ml,lcsk->mcsk", forward, rhs[0], precision=high)
    damped = modal_part / (1.0 + celerity[:, None, None, None] * laplace_eigen)
    divergence = jnp.einsum("kp,phli->khli", back, damped, precision=high)
    temperature = rhs[1] - jnp.einsum("kp,phli->khli", thermal, divergence, precision=high)
    pile = jnp.concatenate([divergence[None], temperature[None], rhs[2:]], 0)
    return jnp.where(inside, pile, jnp.zeros_like(pile)).astype(jnp.bfloat16)


def per_device_plain(rhs, azimuthal, arrangement, polar, forward, back, celerity, thermal):
    fields, levels = rhs.shape[:2]
    slots, nlat, waves = polar.shape
    lat_dev = nlat // lax.axis_size("lat")
    labels = lax.dynamic_slice_in_dim(azimuthal, lax.axis_index("lat") * slots, slots)
    coeffs = implicit_update_quantities(rhs, labels, forward, back, celerity, thermal)
    rows = fields * levels
    natural = jnp.einsum(
        "rsk,slk->rsl",
        coeffs.reshape(rows * 2, slots, waves),
        polar,
        preferred_element_type=jnp.float32,
    )
    fourier = jnp.take(natural, arrangement, axis=2).astype(jnp.bfloat16)
    fourier = fourier.reshape(rows, 2, slots, nlat)
    grid_out = jnp.einsum(
        "icsr,csj->irj",
        lax.all_to_all(fourier, "lat", split_axis=3, concat_axis=2, tiled=True),
        wave_table(azimuthal, NLON),
        preferred_element_type=jnp.float32,
    ).astype(jnp.bfloat16)
    return grid_out.reshape(fields, levels, lat_dev, NLON)


def legendre_kernel(
    azim_ref, arr_ref, fwd_ref, back_ref, cel_ref, therm_ref, rhs_ref, polar_ref, out_ref,
    nat_ref, pad_ref, *, levels, slots, nlat, waves
):
    tiles = waves // LANES
    rows = rhs_ref.shape[0]
    pitch = row_pitch()
    apart = slot_pitch(nlat)
    step = pl.program_id(0)

    def rhs(row, t):
        return rhs_ref[row, :, t * LANES : (t + 1) * LANES]

    first = lax.axis_index("lat") * slots + step * SUBLANES
    sub = lax.broadcasted_iota(jnp.int32, (SUBLANES, LANES), 0)
    lane = lax.broadcasted_iota(jnp.int32, (SUBLANES, LANES), 1)
    label = jnp.zeros((SUBLANES, LANES), jnp.int32)
    for s in range(SUBLANES):
        label = jnp.where(sub == s, azim_ref[first + s], label)

    for group in range(0, tiles, GROUP):
        ts = list(range(group, min(group + GROUP, tiles)))
        parts = [(t, c) for t in ts for c in range(2)]
        span = range(len(parts))

        def mix(matrix, row, operand):
            acc = [matrix[row, 0] * operand[0][i] for i in span]
            for q in range(1, levels):
                acc = [acc[i] + matrix[row, q] * operand[q][i] for i in span]
            return acc

        laplace = []
        for t in ts:
            degree = (label + lane + t * LANES).astype(jnp.float32)
            laplace.append(degree * (degree + 1.0))
        x0 = [[rhs(l * 2 + c, t) for t, c in parts] for l in range(levels)]
        damped = []
        for m in range(levels):
            modal = mix(fwd_ref, m, x0)
            den = [1.0 / (1.0 + cel_ref[m] * lap) for lap in laplace]
            damped.append([modal[i] * den[i // 2] for i in span])
        div = []
        for l in range(levels):
            div.append(mix(back_ref, l, damped))
            for i, (t, c) in enumerate(parts):
                pad_ref[t, pl.ds((l * 2 + c) * pitch, SUBLANES), :] = div[l][i]
        for l in range(levels):
            response = mix(therm_ref, l, div)
            for i, (t, c) in enumerate(parts):
                row = (levels + l) * 2 + c
                pad_ref[t, pl.ds(row * pitch, SUBLANES), :] = rhs(row, t) - response[i]

    for t in range(tiles):
        for row in range(4 * levels, rows):
            pad_ref[t, pl.ds(row * pitch, SUBLANES), :] = rhs(row, t)

    for s in range(SUBLANES):
        room = waves - azim_ref[first + s]
        pieces = []
        for t in range(tiles):
            piece = jnp.concatenate(
                [pad_ref[t, pl.ds(c * pitch + s, rows // 2, stride=2 * pitch), :] for c in range(2)],
                0,
            )
            k = lax.broadcasted_iota(jnp.int32, piece.shape, 1) + t * LANES
            pieces.append(jnp.where(k < room, piece, 0.0).astype(jnp.bfloat16))
        coeffs = jnp.concatenate(pieces, 1)
        product = lax.dot_general(
            polar_ref[s], coeffs, (((1,), (1,)), ((), ())), preferred_element_type=jnp.float32
        )
        nat_ref[pl.ds(s * apart, nlat), :] = product

    half = LANES // 2
    low = lane < half
    pairs = out_ref.shape[1] // (2 * SUBLANES)
    for p in range(nlat // 2):
        a = nat_ref[pl.ds(arr_ref[2 * p], SUBLANES, stride=apart), :]
        b = nat_ref[pl.ds(arr_ref[2 * p + 1], SUBLANES, stride=apart), :]
        real = jnp.where(low, a, pltpu.roll(b, half, 1))
        imag = jnp.where(low, pltpu.roll(a, half, 1), b)
        out_ref[p // pairs, pl.ds(p % pairs * 2 * SUBLANES, 2 * SUBLANES), :] = jnp.concatenate(
            [real, imag], 0
        ).astype(jnp.bfloat16)


def row_pitch():
    return SUBLANES + 1


def slot_pitch(nlat):
    return nlat + 4


def legendre(rhs, azimuthal, arrangement, polar, forward, back, celerity, thermal):
    fields, levels = rhs.shape[:2]
    slots, nlat, waves = polar.shape
    rows = fields * levels * 2
    tiles = waves // LANES
    devices = lax.axis_size("lat")
    steps = slots // SUBLANES
    depth = nlat // devices * SUBLANES
    scalars = (azimuthal, arrangement, forward, back, celerity, thermal)
    return pl.pallas_call(
        functools.partial(
            legendre_kernel, levels=levels, slots=slots, nlat=nlat, waves=waves
        ),
        grid=(steps,),
        in_specs=[pl.BlockSpec(memory_space=pltpu.SMEM)] * len(scalars)
        + [
            pl.BlockSpec((rows, SUBLANES, waves), lambda i: (0, i, 0)),
            pl.BlockSpec((SUBLANES, nlat, waves), lambda i: (i, 0, 0)),
        ],
        out_specs=pl.BlockSpec((devices, None, depth, LANES), lambda i: (0, i, 0, 0)),
        out_shape=jax.ShapeDtypeStruct((devices, steps, depth, LANES), jnp.bfloat16),
        scratch_shapes=[
            pltpu.VMEM((SUBLANES * slot_pitch(nlat), LANES), jnp.float32),
            pltpu.VMEM((tiles, rows * row_pitch(), LANES), jnp.float32),
        ],
        compiler_params=pltpu.CompilerParams(vmem_limit_bytes=60 * 1024 * 1024),
        name="legendre",
    )(*scalars, rhs.reshape(rows, slots, waves), polar)


def table_kernel(azim_ref, cos_ref, sin_ref, *, nlon):
    blocks = nlon // LANES
    m = azim_ref[...]
    lane = lax.broadcasted_iota(jnp.int32, m.shape, 1)
    unit = full_circle_radians / nlon
    fine = ((m * lane) % nlon).astype(jnp.float32) * unit
    coarse = ((m * lane) % blocks).astype(jnp.float32) * (unit * LANES)
    weight = jnp.where(m == 0, 1.0, 2.0)
    cos_fine = weight * jnp.cos(fine)
    sin_fine = weight * jnp.sin(fine)
    cos_coarse = jnp.cos(coarse)
    sin_coarse = jnp.sin(coarse)
    for b in range(blocks // 2 + 1):
        cc = cos_coarse[:, b : b + 1]
        sc = sin_coarse[:, b : b + 1]
        at = slice(b * LANES, (b + 1) * LANES)
        cos_ref[:, at] = (cos_fine * cc - sin_fine * sc).astype(jnp.bfloat16)
        if b < blocks // 2:
            sin_ref[:, at] = (-(sin_fine * cc + cos_fine * sc)).astype(jnp.bfloat16)


def table(azimuthal, rows):
    count = azimuthal.shape[0]
    half = NLON // 2
    spread = jnp.broadcast_to(azimuthal[:, None], (count, LANES))
    return pl.pallas_call(
        functools.partial(table_kernel, nlon=NLON),
        grid=(count // rows,),
        in_specs=[pl.BlockSpec((rows, LANES), lambda d: (d, 0))],
        out_specs=[
            pl.BlockSpec((rows, half + LANES), lambda d: (d, 0)),
            pl.BlockSpec((rows, half), lambda d: (d, 0)),
        ],
        out_shape=[
            jax.ShapeDtypeStruct((count, half + LANES), jnp.bfloat16),
            jax.ShapeDtypeStruct((count, half), jnp.bfloat16),
        ],
        compiler_params=pltpu.CompilerParams(vmem_limit_bytes=16 * 1024 * 1024),
        name="table",
    )(spread)


def grid_kernel(
    x_ref, cos_hbm, sin_hbm, out_hbm, cos_ref, sin_ref, real_ref, imag_ref, out_ref,
    cos_sem, sin_sem, out_sem, *, fields, lat_dev, block,
):
    depth, width = sin_ref.shape
    nlon = 2 * width
    half = LANES // 2
    levels = half // fields
    order = list(range(width // block))[::-1]

    def span(i):
        return pl.ds(i * block, block)

    tail = pl.ds(width, LANES)
    ends = pltpu.make_async_copy(
        cos_hbm.at[:, tail], cos_ref.at[:, tail], cos_sem.at[len(order)]
    )
    loads = {}
    ends.start()
    for i in order:
        loads[i] = [
            pltpu.make_async_copy(cos_hbm.at[:, span(i)], cos_ref.at[:, span(i)], cos_sem.at[i]),
            pltpu.make_async_copy(sin_hbm.at[:, span(i)], sin_ref.at[:, span(i)], sin_sem.at[i]),
        ]
        for copy in loads[i]:
            copy.start()

    for p in range(lat_dev // 2):
        rows = x_ref[:, :, p].astype(jnp.float32)
        for c, ref in enumerate((real_ref, imag_ref)):
            part = rows[:, :, c * SUBLANES : (c + 1) * SUBLANES].reshape(depth, LANES)
            ref[pl.ds(p * LANES, LANES), :] = part.astype(jnp.bfloat16).T

    lane = lax.broadcasted_iota(jnp.int32, (lat_dev * half, LANES), 1)
    mirror = (LANES - lane) % LANES
    ends.wait()
    after = jnp.dot(real_ref[...], cos_ref[:, tail], preferred_element_type=jnp.float32)
    stores = []
    for n, i in enumerate(order):
        for copy in loads[i]:
            copy.wait()
        even = jnp.dot(real_ref[...], cos_ref[:, span(i)], preferred_element_type=jnp.float32)
        odd = jnp.dot(imag_ref[...], sin_ref[:, span(i)], preferred_element_type=jnp.float32)
        near = even + odd
        far = even - odd
        tiles = block // LANES
        parts = [far[:, t * LANES : (t + 1) * LANES] for t in range(tiles)] + [after]
        turned = [
            jnp.where(lane == 0, parts[t + 1], jnp.take_along_axis(parts[t], mirror, axis=1))
            for t in range(tiles)
        ]
        after = parts[0]
        for q, value in enumerate((near, jnp.concatenate(turned[::-1], 1))):
            for r in range(lat_dev):
                for f in range(fields):
                    row = r * half + f * levels
                    out_ref[n, q, f, r] = value[row : row + levels].astype(jnp.bfloat16)
            start = i * block if q == 0 else nlon - (i + 1) * block
            stores.append(
                pltpu.make_async_copy(
                    out_ref.at[n, q], out_hbm.at[:, :, :, pl.ds(start, block)], out_sem.at[n, q]
                )
            )
            stores[-1].start()
    for copy in stores:
        copy.wait()


def grid_product(received, cos, sin, lat_dev, fields, block=256):
    devices, steps = received.shape[:2]
    depth, width = sin.shape
    half = LANES // 2
    levels = half // fields
    count = width // block
    x = received.reshape(devices, steps, lat_dev // 2, 2 * SUBLANES, LANES)
    hbm = pl.BlockSpec(memory_space=pltpu.HBM)
    out = pl.pallas_call(
        functools.partial(grid_kernel, fields=fields, lat_dev=lat_dev, block=block),
        in_specs=[pl.BlockSpec(memory_space=pltpu.VMEM), hbm, hbm],
        out_specs=hbm,
        out_shape=jax.ShapeDtypeStruct((fields, lat_dev, levels, 2 * width), jnp.bfloat16),
        scratch_shapes=[
            pltpu.VMEM(cos.shape, jnp.bfloat16),
            pltpu.VMEM(sin.shape, jnp.bfloat16),
            pltpu.VMEM((lat_dev * half, depth), jnp.bfloat16),
            pltpu.VMEM((lat_dev * half, depth), jnp.bfloat16),
            pltpu.VMEM((count, 2, fields, lat_dev, levels, block), jnp.bfloat16),
            pltpu.SemaphoreType.DMA((count + 1,)),
            pltpu.SemaphoreType.DMA((count,)),
            pltpu.SemaphoreType.DMA((count, 2)),
        ],
        compiler_params=pltpu.CompilerParams(vmem_limit_bytes=40 * 1024 * 1024),
        name="grid_product",
    )(x, *(pltpu.with_memory_space_constraint(a, pltpu.HBM) for a in (cos, sin)))
    return jnp.swapaxes(out, 1, 2)


def per_device(rhs, azimuthal, arrangement, polar, forward, back, celerity, thermal):
    fields, levels = rhs.shape[:2]
    slots, nlat, waves = polar.shape
    devices = lax.axis_size("lat")
    lat_dev = nlat // devices
    packed = legendre(rhs, azimuthal, arrangement, polar, forward, back, celerity, thermal)
    received = lax.all_to_all(packed, "lat", split_axis=0, concat_axis=0, tiled=True)
    cos, sin = table(azimuthal, 2 * slots)
    return grid_product(received, cos, sin, lat_dev, fields)


def solution(mesh):
    in_specs = (
        P("groups", None, None, "lat", None),
        P(),
        P(),
        P("lat", None, None),
        P(),
        P(),
        P(),
        P(),
    )
    out_specs = P("groups", None, "lat", None)

    def body(rhs, azimuthal, arrangement, polar, *matrices):
        slots, nlat, waves = polar.shape
        lat_dev = nlat // lax.axis_size("lat")
        fits = (
            slots % SUBLANES == 0
            and waves % LANES == 0
            and lat_dev % 2 == 0
            and 2 * rhs.shape[0] * rhs.shape[1] == LANES
            and rhs.shape[0] > 2
        )
        form = per_device if fits else per_device_plain
        return form(rhs, azimuthal, arrangement, polar, *matrices)

    return jax.shard_map(
        body, mesh=mesh, in_specs=in_specs, out_specs=out_specs, check_vma=False
    )
```

```python
import functools
import jax
import jax.numpy as jnp
from jax import lax
from jax.experimental import pallas as pl
from jax.experimental.pallas import tpu as pltpu
from jax.sharding import PartitionSpec as P

NLON = 2560
LANES = 128
SUBLANES = 8
GROUP = 2
EARLY = 2
NEAR = 4

full_circle_radians = 6.283185307179586


def wave_table(azimuthal_number_list, nlon):
    longitude = jnp.arange(nlon, dtype=jnp.int32)
    coupled_product = azimuthal_number_list[:, None] * longitude[None, :] % nlon
    phase_angle = coupled_product.astype(jnp.float32) * (full_circle_radians / nlon)
    weight = jnp.where(azimuthal_number_list == 0, 1.0, 2.0).astype(jnp.float32)[:, None]
    return jnp.stack([weight * jnp.cos(phase_angle), -weight * jnp.sin(phase_angle)], 0).astype(
        jnp.bfloat16
    )


def implicit_update_quantities(rhs, position_labels, forward, back, celerity, thermal):
    offsets = jnp.arange(rhs.shape[-1], dtype=jnp.int32)
    total_n = position_labels[:, None] + offsets[None, :]
    inside = total_n < rhs.shape[-1]
    degree = total_n.astype(jnp.float32)
    laplace_eigen = degree * (degree + 1.0)
    high = lax.Precision.HIGHEST
    modal_part = jnp.einsum("ml,lcsk->mcsk", forward, rhs[0], precision=high)
    damped = modal_part / (1.0 + celerity[:, None, None, None] * laplace_eigen)
    divergence = jnp.einsum("kp,phli->khli", back, damped, precision=high)
    temperature = rhs[1] - jnp.einsum("kp,phli->khli", thermal, divergence, precision=high)
    pile = jnp.concatenate([divergence[None], temperature[None], rhs[2:]], 0)
    return jnp.where(inside, pile, jnp.zeros_like(pile)).astype(jnp.bfloat16)


def per_device_plain(rhs, azimuthal, arrangement, polar, forward, back, celerity, thermal):
    fields, levels = rhs.shape[:2]
    slots, nlat, waves = polar.shape
    lat_dev = nlat // lax.axis_size("lat")
    labels = lax.dynamic_slice_in_dim(azimuthal, lax.axis_index("lat") * slots, slots)
    coeffs = implicit_update_quantities(rhs, labels, forward, back, celerity, thermal)
    rows = fields * levels
    natural = jnp.einsum(
        "rsk,slk->rsl",
        coeffs.reshape(rows * 2, slots, waves),
        polar,
        preferred_element_type=jnp.float32,
    )
    fourier = jnp.take(natural, arrangement, axis=2).astype(jnp.bfloat16)
    fourier = fourier.reshape(rows, 2, slots, nlat)
    grid_out = jnp.einsum(
        "icsr,csj->irj",
        lax.all_to_all(fourier, "lat", split_axis=3, concat_axis=2, tiled=True),
        wave_table(azimuthal, NLON),
        preferred_element_type=jnp.float32,
    ).astype(jnp.bfloat16)
    return grid_out.reshape(fields, levels, lat_dev, NLON)


def legendre_kernel(
    azim_ref, arr_ref, fwd_ref, back_ref, cel_ref, therm_ref, rhs_ref, polar_ref, *refs,
    levels, slots, nlat, waves, begin, near
):
    tiles = waves // LANES
    out_refs, (nat_ref, pad_ref) = refs[:-2], refs[-2:]
    rows = rhs_ref.shape[0]
    pitch = row_pitch()
    apart = slot_pitch(nlat)
    step = pl.program_id(0)

    def rhs(row, t):
        return rhs_ref[row, :, t * LANES : (t + 1) * LANES]

    mine = lax.axis_index("lat")
    first = mine * slots + (begin + step) * SUBLANES
    sub = lax.broadcasted_iota(jnp.int32, (SUBLANES, LANES), 0)
    lane = lax.broadcasted_iota(jnp.int32, (SUBLANES, LANES), 1)
    label = jnp.zeros((SUBLANES, LANES), jnp.int32)
    for s in range(SUBLANES):
        label = jnp.where(sub == s, azim_ref[first + s], label)

    for group in range(0, tiles, GROUP):
        ts = list(range(group, min(group + GROUP, tiles)))
        parts = [(t, c) for t in ts for c in range(2)]
        span = range(len(parts))

        def mix(matrix, row, operand):
            acc = [matrix[row, 0] * operand[0][i] for i in span]
            for q in range(1, levels):
                acc = [acc[i] + matrix[row, q] * operand[q][i] for i in span]
            return acc

        laplace = []
        for t in ts:
            degree = (label + lane + t * LANES).astype(jnp.float32)
            laplace.append(degree * (degree + 1.0))
        x0 = [[rhs(l * 2 + c, t) for t, c in parts] for l in range(levels)]
        damped = []
        for m in range(levels):
            modal = mix(fwd_ref, m, x0)
            den = [1.0 / (1.0 + cel_ref[m] * lap) for lap in laplace]
            damped.append([modal[i] * den[i // 2] for i in span])
        div = []
        for l in range(levels):
            div.append(mix(back_ref, l, damped))
            for i, (t, c) in enumerate(parts):
                pad_ref[t, pl.ds((l * 2 + c) * pitch, SUBLANES), :] = div[l][i]
        for l in range(levels):
            response = mix(therm_ref, l, div)
            for i, (t, c) in enumerate(parts):
                row = (levels + l) * 2 + c
                pad_ref[t, pl.ds(row * pitch, SUBLANES), :] = rhs(row, t) - response[i]

    for t in range(tiles):
        for row in range(4 * levels, rows):
            pad_ref[t, pl.ds(row * pitch, SUBLANES), :] = rhs(row, t)

    for s in range(SUBLANES):
        room = waves - azim_ref[first + s]
        pieces = []
        for t in range(tiles):
            piece = jnp.concatenate(
                [pad_ref[t, pl.ds(c * pitch + s, rows // 2, stride=2 * pitch), :] for c in range(2)],
                0,
            )
            k = lax.broadcasted_iota(jnp.int32, piece.shape, 1) + t * LANES
            pieces.append(jnp.where(k < room, piece, 0.0).astype(jnp.bfloat16))
        coeffs = jnp.concatenate(pieces, 1)
        product = lax.dot_general(
            polar_ref[s], coeffs, (((1,), (1,)), ((), ())), preferred_element_type=jnp.float32
        )
        nat_ref[pl.ds(s * apart, nlat), :] = product

    half = LANES // 2
    low = lane < half
    pairs = out_refs[0].shape[1] // (2 * SUBLANES)
    for p in range(nlat // 2):
        d, q = divmod(p, pairs)
        at = ((mine ^ d if near else d) * pairs + q) * 2
        a = nat_ref[pl.ds(arr_ref[at], SUBLANES, stride=apart), :]
        b = nat_ref[pl.ds(arr_ref[at + 1], SUBLANES, stride=apart), :]
        real = jnp.where(low, a, pltpu.roll(b, half, 1))
        imag = jnp.where(low, pltpu.roll(a, half, 1), b)
        group, place = divmod(d, out_refs[0].shape[0])
        out_refs[group][place, pl.ds(q * 2 * SUBLANES, 2 * SUBLANES), :] = jnp.concatenate(
            [real, imag], 0
        ).astype(jnp.bfloat16)


def row_pitch():
    return SUBLANES + 1


def slot_pitch(nlat):
    return nlat + 4


def legendre(
    rhs, azimuthal, arrangement, polar, forward, back, celerity, thermal, begin, steps, near=0
):
    fields, levels = rhs.shape[:2]
    slots, nlat, waves = polar.shape
    rows = fields * levels * 2
    tiles = waves // LANES
    devices = lax.axis_size("lat")
    depth = nlat // devices * SUBLANES
    scalars = (azimuthal, arrangement, forward, back, celerity, thermal)
    group = near or devices
    outs = devices // group
    return pl.pallas_call(
        functools.partial(
            legendre_kernel,
            levels=levels, slots=slots, nlat=nlat, waves=waves, begin=begin, near=near,
        ),
        grid=(steps,),
        in_specs=[pl.BlockSpec(memory_space=pltpu.SMEM)] * len(scalars)
        + [
            pl.BlockSpec((rows, SUBLANES, waves), lambda i: (0, begin + i, 0)),
            pl.BlockSpec((SUBLANES, nlat, waves), lambda i: (begin + i, 0, 0)),
        ],
        out_specs=[pl.BlockSpec((group, None, depth, LANES), lambda i: (0, i, 0, 0))] * outs,
        out_shape=[jax.ShapeDtypeStruct((group, steps, depth, LANES), jnp.bfloat16)] * outs,
        scratch_shapes=[
            pltpu.VMEM((SUBLANES * slot_pitch(nlat), LANES), jnp.float32),
            pltpu.VMEM((tiles, rows * row_pitch(), LANES), jnp.float32),
        ],
        compiler_params=pltpu.CompilerParams(vmem_limit_bytes=60 * 1024 * 1024),
        name="legendre",
    )(*scalars, rhs.reshape(rows, slots, waves), polar)


def table_rows(m, cos_ref, sin_ref, nlon):
    blocks = nlon // LANES
    lane = lax.broadcasted_iota(jnp.int32, m.shape, 1)
    unit = full_circle_radians / nlon
    fine = ((m * lane) % nlon).astype(jnp.float32) * unit
    coarse = ((m * lane) % blocks).astype(jnp.float32) * (unit * LANES)
    weight = jnp.where(m == 0, 1.0, 2.0)
    cos_fine = weight * jnp.cos(fine)
    sin_fine = weight * jnp.sin(fine)
    cos_coarse = jnp.cos(coarse)
    sin_coarse = jnp.sin(coarse)
    for b in range(blocks // 2 + 1):
        cc = cos_coarse[:, b : b + 1]
        sc = sin_coarse[:, b : b + 1]
        at = slice(b * LANES, (b + 1) * LANES)
        cos_ref[:, at] = (cos_fine * cc - sin_fine * sc).astype(jnp.bfloat16)
        if b < blocks // 2:
            sin_ref[:, at] = (-(sin_fine * cc + cos_fine * sc)).astype(jnp.bfloat16)


def table_kernel(azim_ref, *refs, nlon, early, near):
    step = pl.program_id(0)
    mine = lax.axis_index("lat")
    devices = azim_ref.shape[0]
    groups = devices // near
    ones, others = [], []
    for i in range(2):
        d = 2 * step + i
        ones.append(azim_ref[mine ^ (d % groups * near + d // groups), :early])
        others.append(azim_ref[d, early:])
    table_rows(jnp.concatenate(ones, 0), refs[0], refs[1], nlon)
    table_rows(jnp.concatenate(others, 0), refs[2], refs[3], nlon)


def tables(azimuthal, devices, early, near):
    slots = azimuthal.shape[0] // devices
    half = NLON // 2
    spread = jnp.broadcast_to(azimuthal.reshape(devices, slots, 1), (devices, slots, LANES))
    widths = (half + LANES, half) * 2
    counts = (early, early, slots - early, slots - early)
    return pl.pallas_call(
        functools.partial(table_kernel, nlon=NLON, early=early, near=near),
        grid=(devices // 2,),
        in_specs=[pl.BlockSpec(memory_space=pltpu.VMEM)],
        out_specs=[pl.BlockSpec((2 * n, w), lambda d: (d, 0)) for n, w in zip(counts, widths)],
        out_shape=[
            jax.ShapeDtypeStruct((devices * n, w), jnp.bfloat16) for n, w in zip(counts, widths)
        ],
        compiler_params=pltpu.CompilerParams(vmem_limit_bytes=16 * 1024 * 1024),
        name="tables",
    )(spread)


def grid_kernel(
    *refs, near, fields, lat_dev, block
):
    early_refs, late_ref, tables, out_hbm = refs[:near], refs[near], refs[near + 1 : near + 5], refs[near + 5]
    cos_ref, sin_ref, real_ref, imag_ref, out_ref, load_sem, out_sem = refs[near + 6 :]
    width = sin_ref.shape[1]
    early = tables[0].shape[0]
    nlon = 2 * width
    half = LANES // 2
    levels = half // fields
    order = list(range(width // block))[::-1]

    def span(i):
        return pl.ds(i * block, block)

    def load(i, columns, which):
        copies = []
        for n in which:
            ref = (cos_ref, sin_ref)[n % 2]
            rows = pl.ds(n // 2 * early, tables[n].shape[0])
            copies.append(
                pltpu.make_async_copy(
                    tables[n].at[:, columns], ref.at[rows, columns], load_sem.at[i, n]
                )
            )
            copies[-1].start()
        return copies

    tail = pl.ds(width, LANES)
    ends = load(len(order), tail, (0, 2))
    loads = {i: load(i, span(i), range(4)) for i in order}

    for p in range(lat_dev // 2):
        first = jnp.concatenate([ref[:, :, p] for ref in early_refs], 0).astype(jnp.float32)
        later = late_ref[:, :, p].astype(jnp.float32)
        at = 0
        for rows in (first, later):
            count = rows.shape[0] * rows.shape[1] * SUBLANES
            for c, ref in enumerate((real_ref, imag_ref)):
                part = rows[:, :, c * SUBLANES : (c + 1) * SUBLANES].reshape(count, LANES)
                ref[pl.ds(p * LANES, LANES), pl.ds(at, count)] = part.astype(jnp.bfloat16).T
            at += count

    lane = lax.broadcasted_iota(jnp.int32, (lat_dev * half, LANES), 1)
    mirror = (LANES - lane) % LANES
    for copy in ends:
        copy.wait()
    after = jnp.dot(real_ref[...], cos_ref[:, tail], preferred_element_type=jnp.float32)
    stores = []
    for n, i in enumerate(order):
        for copy in loads[i]:
            copy.wait()
        even = jnp.dot(real_ref[...], cos_ref[:, span(i)], preferred_element_type=jnp.float32)
        odd = jnp.dot(imag_ref[...], sin_ref[:, span(i)], preferred_element_type=jnp.float32)
        near = even + odd
        far = even - odd
        tiles = block // LANES
        parts = [far[:, t * LANES : (t + 1) * LANES] for t in range(tiles)] + [after]
        turned = [
            jnp.where(lane == 0, parts[t + 1], jnp.take_along_axis(parts[t], mirror, axis=1))
            for t in range(tiles)
        ]
        after = parts[0]
        for q, value in enumerate((near, jnp.concatenate(turned[::-1], 1))):
            for r in range(lat_dev):
                for f in range(fields):
                    row = r * half + f * levels
                    out_ref[n, q, f, r] = value[row : row + levels].astype(jnp.bfloat16)
            start = i * block if q == 0 else nlon - (i + 1) * block
            stores.append(
                pltpu.make_async_copy(
                    out_ref.at[n, q], out_hbm.at[:, :, :, pl.ds(start, block)], out_sem.at[n, q]
                )
            )
            stores[-1].start()
    for copy in stores:
        copy.wait()


def grid_product(early, late, tabs, lat_dev, fields, block=256):
    near = len(early)
    width = tabs[1].shape[1]
    depth = tabs[1].shape[0] + tabs[3].shape[0]
    half = LANES // 2
    levels = half // fields
    count = width // block
    parts = [
        x.reshape(*x.shape[:2], lat_dev // 2, 2 * SUBLANES, LANES) for x in (*early, late)
    ]
    hbm = pl.BlockSpec(memory_space=pltpu.HBM)
    out = pl.pallas_call(
        functools.partial(grid_kernel, near=near, fields=fields, lat_dev=lat_dev, block=block),
        in_specs=[pl.BlockSpec(memory_space=pltpu.VMEM)] * len(parts) + [hbm] * len(tabs),
        out_specs=hbm,
        out_shape=jax.ShapeDtypeStruct((fields, lat_dev, levels, 2 * width), jnp.bfloat16),
        scratch_shapes=[
            pltpu.VMEM((depth, width + LANES), jnp.bfloat16),
            pltpu.VMEM((depth, width), jnp.bfloat16),
            pltpu.VMEM((lat_dev * half, depth), jnp.bfloat16),
            pltpu.VMEM((lat_dev * half, depth), jnp.bfloat16),
            pltpu.VMEM((count, 2, fields, lat_dev, levels, block), jnp.bfloat16),
            pltpu.SemaphoreType.DMA((count + 1, len(tabs))),
            pltpu.SemaphoreType.DMA((count, 2)),
        ],
        compiler_params=pltpu.CompilerParams(vmem_limit_bytes=40 * 1024 * 1024),
        name="grid_product",
    )(*parts, *(pltpu.with_memory_space_constraint(a, pltpu.HBM) for a in tabs))
    return jnp.swapaxes(out, 1, 2)


def per_device(rhs, azimuthal, arrangement, polar, forward, back, celerity, thermal):
    fields = rhs.shape[0]
    slots, nlat, _ = polar.shape
    devices = lax.axis_size("lat")
    lat_dev = nlat // devices
    steps = slots // SUBLANES
    operands = (rhs, azimuthal, arrangement, polar, forward, back, celerity, thermal)

    def swap(x, distance):
        return lax.ppermute(x, "lat", [(d, d ^ distance) for d in range(devices)])

    mine = legendre(*operands, 0, EARLY, NEAR)
    got = [mine[0]]
    for g in range(1, devices // NEAR):
        got.append(swap(mine[g], g * NEAR))
    (packed,) = legendre(*operands, EARLY, steps - EARLY)
    late = lax.all_to_all(packed, "lat", split_axis=0, concat_axis=0, tiled=True)
    early = []
    for j in range(NEAR):
        part = jnp.concatenate([x[j : j + 1] for x in got], 0)
        early.append(swap(part, j) if j else part)
    tabs = tables(azimuthal, devices, EARLY * SUBLANES, NEAR)
    return grid_product(early, late, tabs, lat_dev, fields)


def solution(mesh):
    in_specs = (
        P("groups", None, None, "lat", None),
        P(),
        P(),
        P("lat", None, None),
        P(),
        P(),
        P(),
        P(),
    )
    out_specs = P("groups", None, "lat", None)

    def body(rhs, azimuthal, arrangement, polar, *matrices):
        slots, nlat, waves = polar.shape
        lat_dev = nlat // lax.axis_size("lat")
        fits = (
            slots % SUBLANES == 0
            and waves % LANES == 0
            and lat_dev % 2 == 0
            and 2 * rhs.shape[0] * rhs.shape[1] == LANES
            and rhs.shape[0] > 2
            and slots // SUBLANES > EARLY
            and lax.axis_size("lat") % NEAR == 0
            and lax.axis_size("lat") & (lax.axis_size("lat") - 1) == 0
        )
        form = per_device if fits else per_device_plain
        return form(rhs, azimuthal, arrangement, polar, *matrices)

    return jax.shard_map(
        body, mesh=mesh, in_specs=in_specs, out_specs=out_specs, check_vma=False
    )
```

```python
import functools
import jax
import jax.numpy as jnp
from jax import lax
from jax.experimental import pallas as pl
from jax.experimental.pallas import tpu as pltpu
from jax.sharding import PartitionSpec as P

NLON = 2560
LANES = 128
SUBLANES = 8
GROUP = 2
VMEM_MIB = 40
EARLY = 2
NEAR = 4

full_circle_radians = 6.283185307179586


def wave_table(azimuthal_number_list, nlon):
    longitude = jnp.arange(nlon, dtype=jnp.int32)
    coupled_product = azimuthal_number_list[:, None] * longitude[None, :] % nlon
    phase_angle = coupled_product.astype(jnp.float32) * (full_circle_radians / nlon)
    weight = jnp.where(azimuthal_number_list == 0, 1.0, 2.0).astype(jnp.float32)[:, None]
    return jnp.stack([weight * jnp.cos(phase_angle), -weight * jnp.sin(phase_angle)], 0).astype(
        jnp.bfloat16
    )


def implicit_update_quantities(rhs, position_labels, forward, back, celerity, thermal):
    offsets = jnp.arange(rhs.shape[-1], dtype=jnp.int32)
    total_n = position_labels[:, None] + offsets[None, :]
    inside = total_n < rhs.shape[-1]
    degree = total_n.astype(jnp.float32)
    laplace_eigen = degree * (degree + 1.0)
    high = lax.Precision.HIGHEST
    modal_part = jnp.einsum("ml,lcsk->mcsk", forward, rhs[0], precision=high)
    damped = modal_part / (1.0 + celerity[:, None, None, None] * laplace_eigen)
    divergence = jnp.einsum("kp,phli->khli", back, damped, precision=high)
    temperature = rhs[1] - jnp.einsum("kp,phli->khli", thermal, divergence, precision=high)
    pile = jnp.concatenate([divergence[None], temperature[None], rhs[2:]], 0)
    return jnp.where(inside, pile, jnp.zeros_like(pile)).astype(jnp.bfloat16)


def per_device_plain(rhs, azimuthal, arrangement, polar, forward, back, celerity, thermal):
    fields, levels = rhs.shape[:2]
    slots, nlat, waves = polar.shape
    lat_dev = nlat // lax.axis_size("lat")
    labels = lax.dynamic_slice_in_dim(azimuthal, lax.axis_index("lat") * slots, slots)
    coeffs = implicit_update_quantities(rhs, labels, forward, back, celerity, thermal)
    rows = fields * levels
    natural = jnp.einsum(
        "rsk,slk->rsl",
        coeffs.reshape(rows * 2, slots, waves),
        polar,
        preferred_element_type=jnp.float32,
    )
    fourier = jnp.take(natural, arrangement, axis=2).astype(jnp.bfloat16)
    fourier = fourier.reshape(rows, 2, slots, nlat)
    grid_out = jnp.einsum(
        "icsr,csj->irj",
        lax.all_to_all(fourier, "lat", split_axis=3, concat_axis=2, tiled=True),
        wave_table(azimuthal, NLON),
        preferred_element_type=jnp.float32,
    ).astype(jnp.bfloat16)
    return grid_out.reshape(fields, levels, lat_dev, NLON)


def legendre_kernel(
    *refs, levels, begin, steps, near, outs, carried, carry
):
    refs = list(refs)
    sources = [refs.pop(0) for _ in range(6)]
    rhs_hbm, polar_hbm = refs.pop(0), refs.pop(0)
    given = [refs.pop(0) for _ in range(2 * carried)]
    out_hbms = [refs.pop(0) for _ in range(outs)]
    taken = [refs.pop(0) for _ in range(2 * carry)]
    scalars = [refs.pop(0) for _ in range(6)]
    rhs_buf, polar_buf, nat_one, nat_two, pad_one, pad_two, stage_ref = refs[:7]
    scalar_sem, load_sem, out_sem = refs[7:]
    azim_ref, arr_ref, *matrices = scalars

    small = [
        pltpu.make_async_copy(src, dst, scalar_sem.at[i])
        for i, (src, dst) in enumerate(zip(sources, scalars))
    ]
    for copy in small:
        copy.start()

    def load(step, targets):
        at = pl.ds((begin + step) * SUBLANES, SUBLANES)
        copies = [
            pltpu.make_async_copy(rhs_hbm.at[:, at, :], targets[0], load_sem.at[step, 0]),
            pltpu.make_async_copy(polar_hbm.at[at], targets[1], load_sem.at[step, 1]),
        ]
        for copy in copies:
            copy.start()
        return copies

    blocks, loads, stores = {}, {}, []
    for step in range(steps):
        own = step - carried
        blocks[step] = (rhs_buf.at[own], polar_buf.at[own]) if own >= 0 else tuple(given)
    if carry:
        blocks[steps] = tuple(taken)
    for step in range(carried, min(carried + 2, steps)):
        loads[step] = load(step, blocks[step])

    def arrive(step):
        for copy in loads.get(step, ()):
            copy.wait()
        after = step + 2
        if after in blocks and after not in loads:
            loads[after] = load(after, blocks[after])

    def prepare(step):
        pad = (pad_one, pad_two)[step % 2]
        yield from update_parts(azim_ref, matrices, blocks[step][0], pad, begin + step, levels)

    def finish(step):
        pad, nat = ((pad_one, nat_one), (pad_two, nat_two))[step % 2]
        outputs = [stage_ref.at[step, g] for g in range(outs)]
        yield from product_parts(
            azim_ref, arr_ref, blocks[step][1], pad, nat, outputs, begin + step, near
        )
        for g in range(outs):
            stores.append(
                pltpu.make_async_copy(
                    stage_ref.at[step, g], out_hbms[g].at[:, step], out_sem.at[step, g]
                )
            )
            stores[-1].start()

    arrive(0)
    for copy in small:
        copy.wait()
    for _ in prepare(0):
        pass
    for step in range(steps):
        following = iter(())
        if step + 1 < steps and carried:
            arrive(step + 1)
            following = prepare(step + 1)
        for _ in finish(step):
            next(following, None)
        for _ in following:
            pass
        if step + 1 < steps and not carried:
            arrive(step + 1)
            for _ in prepare(step + 1):
                pass
    for copy in loads.get(steps, ()):
        copy.wait()
    for copy in stores:
        copy.wait()


def first_slot(azim_ref, step):
    own = azim_ref.shape[0] // lax.axis_size("lat")
    return lax.axis_index("lat") * own + step * SUBLANES


def update_parts(azim_ref, matrices, rhs_ref, pad_ref, step, levels):
    fwd_ref, back_ref, cel_ref, therm_ref = matrices
    rows, _, waves = rhs_ref.shape
    tiles = waves // LANES
    pitch = row_pitch()
    first = first_slot(azim_ref, step)

    def rhs(row, t):
        return rhs_ref[row, :, t * LANES : (t + 1) * LANES]

    sub = lax.broadcasted_iota(jnp.int32, (SUBLANES, LANES), 0)
    lane = lax.broadcasted_iota(jnp.int32, (SUBLANES, LANES), 1)
    label = jnp.zeros((SUBLANES, LANES), jnp.int32)
    for s in range(SUBLANES):
        label = jnp.where(sub == s, azim_ref[first + s], label)

    for group in range(0, tiles, GROUP):
        ts = list(range(group, min(group + GROUP, tiles)))
        parts = [(t, c) for t in ts for c in range(2)]
        span = range(len(parts))

        def mix(matrix, row, operand):
            acc = [matrix[row, 0] * operand[0][i] for i in span]
            for q in range(1, levels):
                acc = [acc[i] + matrix[row, q] * operand[q][i] for i in span]
            return acc

        laplace = []
        for t in ts:
            degree = (label + lane + t * LANES).astype(jnp.float32)
            laplace.append(degree * (degree + 1.0))
        x0 = [[rhs(l * 2 + c, t) for t, c in parts] for l in range(levels)]
        damped = []
        for m in range(levels):
            modal = mix(fwd_ref, m, x0)
            den = [1.0 / (1.0 + cel_ref[m] * lap) for lap in laplace]
            damped.append([modal[i] * den[i // 2] for i in span])
        div = []
        for l in range(levels):
            div.append(mix(back_ref, l, damped))
            for i, (t, c) in enumerate(parts):
                pad_ref[t, pl.ds((l * 2 + c) * pitch, SUBLANES), :] = div[l][i]
        for l in range(levels):
            response = mix(therm_ref, l, div)
            for i, (t, c) in enumerate(parts):
                row = (levels + l) * 2 + c
                pad_ref[t, pl.ds(row * pitch, SUBLANES), :] = rhs(row, t) - response[i]
        for t in ts:
            for row in range(4 * levels, rows):
                pad_ref[t, pl.ds(row * pitch, SUBLANES), :] = rhs(row, t)
        yield


def product_parts(azim_ref, arr_ref, polar_ref, pad_ref, nat_ref, out_refs, step, near):
    _, nlat, waves = polar_ref.shape
    tiles = waves // LANES
    pitch = row_pitch()
    apart = slot_pitch(nlat)
    rows = pad_ref.shape[1] // pitch
    mine = lax.axis_index("lat")
    first = first_slot(azim_ref, step)
    for s in range(SUBLANES):
        room = waves - azim_ref[first + s]
        pieces = []
        for t in range(tiles):
            piece = jnp.concatenate(
                [pad_ref[t, pl.ds(c * pitch + s, rows // 2, stride=2 * pitch), :] for c in range(2)],
                0,
            )
            k = lax.broadcasted_iota(jnp.int32, piece.shape, 1) + t * LANES
            pieces.append(jnp.where(k < room, piece, 0.0).astype(jnp.bfloat16))
        coeffs = jnp.concatenate(pieces, 1)
        product = lax.dot_general(
            polar_ref[s], coeffs, (((1,), (1,)), ((), ())), preferred_element_type=jnp.float32
        )
        nat_ref[pl.ds(s * apart, nlat), :] = product
        yield

    half = LANES // 2
    low = lax.broadcasted_iota(jnp.int32, (SUBLANES, LANES), 1) < half
    pairs = out_refs[0].shape[1] // (2 * SUBLANES)
    for p in range(nlat // 2):
        d, q = divmod(p, pairs)
        at = ((mine ^ d if near else d) * pairs + q) * 2
        a = nat_ref[pl.ds(arr_ref[at], SUBLANES, stride=apart), :]
        b = nat_ref[pl.ds(arr_ref[at + 1], SUBLANES, stride=apart), :]
        real = jnp.where(low, a, pltpu.roll(b, half, 1))
        imag = jnp.where(low, pltpu.roll(a, half, 1), b)
        group, place = divmod(d, out_refs[0].shape[0])
        out_refs[group][place, pl.ds(q * 2 * SUBLANES, 2 * SUBLANES), :] = jnp.concatenate(
            [real, imag], 0
        ).astype(jnp.bfloat16)
    yield


def row_pitch():
    return SUBLANES + 1


def slot_pitch(nlat):
    return nlat + 4


def legendre(
    rhs, azimuthal, arrangement, polar, forward, back, celerity, thermal, begin, steps,
    near=0, given=(), carry=False,
):
    fields, levels = rhs.shape[:2]
    slots, nlat, waves = polar.shape
    rows = fields * levels * 2
    tiles = waves // LANES
    devices = lax.axis_size("lat")
    depth = nlat // devices * SUBLANES
    scalars = (azimuthal, arrangement, forward, back, celerity, thermal)
    group = near or devices
    outs = devices // group
    carried = len(given) // 2
    hbm = pl.BlockSpec(memory_space=pltpu.HBM)
    vmem = pl.BlockSpec(memory_space=pltpu.VMEM)
    rhs_block, polar_block = (rows, SUBLANES, waves), (SUBLANES, nlat, waves)
    next_blocks = [
        jax.ShapeDtypeStruct(rhs_block, rhs.dtype),
        jax.ShapeDtypeStruct(polar_block, polar.dtype),
    ]
    own = steps - carried
    return pl.pallas_call(
        functools.partial(
            legendre_kernel, levels=levels, begin=begin, steps=steps, near=near, outs=outs,
            carried=carried, carry=int(carry),
        ),
        in_specs=[hbm] * (len(scalars) + 2) + [vmem] * len(given),
        out_specs=[hbm] * outs + [vmem, vmem] * carry,
        out_shape=[jax.ShapeDtypeStruct((group, steps, depth, LANES), jnp.bfloat16)] * outs
        + next_blocks * carry,
        scratch_shapes=[pltpu.SMEM(a.shape, a.dtype) for a in scalars]
        + [
            pltpu.VMEM((own, *rhs_block), rhs.dtype),
            pltpu.VMEM((own, *polar_block), polar.dtype),
        ]
        + [pltpu.VMEM((SUBLANES * slot_pitch(nlat), LANES), jnp.float32)] * 2
        + [pltpu.VMEM((tiles, rows * row_pitch(), LANES), jnp.float32)] * 2
        + [
            pltpu.VMEM((steps, outs, group, depth, LANES), jnp.bfloat16),
            pltpu.SemaphoreType.DMA((len(scalars),)),
            pltpu.SemaphoreType.DMA((steps + 1, 2)),
            pltpu.SemaphoreType.DMA((steps, outs)),
        ],
        compiler_params=pltpu.CompilerParams(vmem_limit_bytes=VMEM_MIB * 1024 * 1024),
        name="legendre",
    )(
        *(pltpu.with_memory_space_constraint(a, pltpu.HBM) for a in scalars),
        pltpu.with_memory_space_constraint(rhs.reshape(rows, slots, waves), pltpu.HBM),
        pltpu.with_memory_space_constraint(polar, pltpu.HBM),
        *(pltpu.with_memory_space_constraint(a, pltpu.VMEM) for a in given),
    )


def table_rows(m, cos_ref, sin_ref, nlon):
    blocks = nlon // LANES
    lane = lax.broadcasted_iota(jnp.int32, m.shape, 1)
    unit = full_circle_radians / nlon
    fine = ((m * lane) % nlon).astype(jnp.float32) * unit
    coarse = ((m * lane) % blocks).astype(jnp.float32) * (unit * LANES)
    weight = jnp.where(m == 0, 1.0, 2.0)
    cos_fine = weight * jnp.cos(fine)
    sin_fine = weight * jnp.sin(fine)
    cos_coarse = jnp.cos(coarse)
    sin_coarse = jnp.sin(coarse)
    for b in range(blocks // 2 + 1):
        cc = cos_coarse[:, b : b + 1]
        sc = sin_coarse[:, b : b + 1]
        at = slice(b * LANES, (b + 1) * LANES)
        cos_ref[:, at] = (cos_fine * cc - sin_fine * sc).astype(jnp.bfloat16)
        if b < blocks // 2:
            sin_ref[:, at] = (-(sin_fine * cc + cos_fine * sc)).astype(jnp.bfloat16)


def table_kernel(azim_ref, *refs, nlon, early, near):
    step = pl.program_id(0)
    mine = lax.axis_index("lat")
    devices = azim_ref.shape[0]
    groups = devices // near
    ones, others = [], []
    for i in range(2):
        d = 2 * step + i
        ones.append(azim_ref[mine ^ (d % groups * near + d // groups), :early])
        others.append(azim_ref[d, early:])
    table_rows(jnp.concatenate(ones, 0), refs[0], refs[1], nlon)
    table_rows(jnp.concatenate(others, 0), refs[2], refs[3], nlon)


def tables(azimuthal, devices, early, near):
    slots = azimuthal.shape[0] // devices
    half = NLON // 2
    spread = jnp.broadcast_to(azimuthal.reshape(devices, slots, 1), (devices, slots, LANES))
    widths = (half + LANES, half) * 2
    counts = (early, early, slots - early, slots - early)
    return pl.pallas_call(
        functools.partial(table_kernel, nlon=NLON, early=early, near=near),
        grid=(devices // 2,),
        in_specs=[pl.BlockSpec(memory_space=pltpu.VMEM)],
        out_specs=[pl.BlockSpec((2 * n, w), lambda d: (d, 0)) for n, w in zip(counts, widths)],
        out_shape=[
            jax.ShapeDtypeStruct((devices * n, w), jnp.bfloat16) for n, w in zip(counts, widths)
        ],
        compiler_params=pltpu.CompilerParams(vmem_limit_bytes=16 * 1024 * 1024),
        name="tables",
    )(spread)


def grid_kernel(
    *refs, near, fields, lat_dev, block
):
    early_refs, late_ref, tables, out_hbm = refs[:near], refs[near], refs[near + 1 : near + 5], refs[near + 5]
    cos_ref, sin_ref, real_ref, imag_ref, out_ref, load_sem, out_sem = refs[near + 6 :]
    width = sin_ref.shape[1]
    early = tables[0].shape[0]
    nlon = 2 * width
    half = LANES // 2
    levels = half // fields
    order = list(range(width // block))[::-1]

    def span(i):
        return pl.ds(i * block, block)

    def load(i, columns, which):
        copies = []
        for n in which:
            ref = (cos_ref, sin_ref)[n % 2]
            rows = pl.ds(n // 2 * early, tables[n].shape[0])
            copies.append(
                pltpu.make_async_copy(
                    tables[n].at[:, columns], ref.at[rows, columns], load_sem.at[i, n]
                )
            )
            copies[-1].start()
        return copies

    tail = pl.ds(width, LANES)
    ends = load(len(order), tail, (0, 2))
    loads = {i: load(i, span(i), range(4)) for i in order}

    for p in range(lat_dev // 2):
        first = jnp.concatenate([ref[:, :, p] for ref in early_refs], 0).astype(jnp.float32)
        later = late_ref[:, :, p].astype(jnp.float32)
        at = 0
        for rows in (first, later):
            count = rows.shape[0] * rows.shape[1] * SUBLANES
            for c, ref in enumerate((real_ref, imag_ref)):
                part = rows[:, :, c * SUBLANES : (c + 1) * SUBLANES].reshape(count, LANES)
                ref[pl.ds(p * LANES, LANES), pl.ds(at, count)] = part.astype(jnp.bfloat16).T
            at += count

    lane = lax.broadcasted_iota(jnp.int32, (lat_dev * half, LANES), 1)
    mirror = (LANES - lane) % LANES
    for copy in ends:
        copy.wait()
    after = jnp.dot(real_ref[...], cos_ref[:, tail], preferred_element_type=jnp.float32)
    stores = []
    for n, i in enumerate(order):
        for copy in loads[i]:
            copy.wait()
        even = jnp.dot(real_ref[...], cos_ref[:, span(i)], preferred_element_type=jnp.float32)
        odd = jnp.dot(imag_ref[...], sin_ref[:, span(i)], preferred_element_type=jnp.float32)
        near = even + odd
        far = even - odd
        tiles = block // LANES
        parts = [far[:, t * LANES : (t + 1) * LANES] for t in range(tiles)] + [after]
        turned = [
            jnp.where(lane == 0, parts[t + 1], jnp.take_along_axis(parts[t], mirror, axis=1))
            for t in range(tiles)
        ]
        after = parts[0]
        for q, value in enumerate((near, jnp.concatenate(turned[::-1], 1))):
            for r in range(lat_dev):
                for f in range(fields):
                    row = r * half + f * levels
                    out_ref[n, q, f, r] = value[row : row + levels].astype(jnp.bfloat16)
            start = i * block if q == 0 else nlon - (i + 1) * block
            stores.append(
                pltpu.make_async_copy(
                    out_ref.at[n, q], out_hbm.at[:, :, :, pl.ds(start, block)], out_sem.at[n, q]
                )
            )
            stores[-1].start()
    for copy in stores:
        copy.wait()


def grid_product(early, late, tabs, lat_dev, fields, block=256):
    near = len(early)
    width = tabs[1].shape[1]
    depth = tabs[1].shape[0] + tabs[3].shape[0]
    half = LANES // 2
    levels = half // fields
    count = width // block
    parts = [
        x.reshape(*x.shape[:2], lat_dev // 2, 2 * SUBLANES, LANES) for x in (*early, late)
    ]
    hbm = pl.BlockSpec(memory_space=pltpu.HBM)
    out = pl.pallas_call(
        functools.partial(grid_kernel, near=near, fields=fields, lat_dev=lat_dev, block=block),
        in_specs=[pl.BlockSpec(memory_space=pltpu.VMEM)] * len(parts) + [hbm] * len(tabs),
        out_specs=hbm,
        out_shape=jax.ShapeDtypeStruct((fields, lat_dev, levels, 2 * width), jnp.bfloat16),
        scratch_shapes=[
            pltpu.VMEM((depth, width + LANES), jnp.bfloat16),
            pltpu.VMEM((depth, width), jnp.bfloat16),
            pltpu.VMEM((lat_dev * half, depth), jnp.bfloat16),
            pltpu.VMEM((lat_dev * half, depth), jnp.bfloat16),
            pltpu.VMEM((count, 2, fields, lat_dev, levels, block), jnp.bfloat16),
            pltpu.SemaphoreType.DMA((count + 1, len(tabs))),
            pltpu.SemaphoreType.DMA((count, 2)),
        ],
        compiler_params=pltpu.CompilerParams(vmem_limit_bytes=40 * 1024 * 1024),
        name="grid_product",
    )(*parts, *(pltpu.with_memory_space_constraint(a, pltpu.HBM) for a in tabs))
    return jnp.swapaxes(out, 1, 2)


def per_device(rhs, azimuthal, arrangement, polar, forward, back, celerity, thermal):
    fields = rhs.shape[0]
    slots, nlat, _ = polar.shape
    devices = lax.axis_size("lat")
    lat_dev = nlat // devices
    steps = slots // SUBLANES
    operands = (rhs, azimuthal, arrangement, polar, forward, back, celerity, thermal)

    def swap(x, distance):
        return lax.ppermute(x, "lat", [(d, d ^ distance) for d in range(devices)])

    *mine, next_rhs, next_polar = legendre(*operands, 0, EARLY, NEAR, carry=True)
    got = [mine[0]]
    for g in range(1, devices // NEAR):
        got.append(swap(mine[g], g * NEAR))
    (packed,) = legendre(
        *operands, EARLY, steps - EARLY, given=(next_rhs, next_polar)
    )
    late = lax.all_to_all(packed, "lat", split_axis=0, concat_axis=0, tiled=True)
    early = []
    for j in range(NEAR):
        part = jnp.concatenate([x[j : j + 1] for x in got], 0)
        early.append(swap(part, j) if j else part)
    tabs = tables(azimuthal, devices, EARLY * SUBLANES, NEAR)
    return grid_product(early, late, tabs, lat_dev, fields)


def solution(mesh):
    in_specs = (
        P("groups", None, None, "lat", None),
        P(),
        P(),
        P("lat", None, None),
        P(),
        P(),
        P(),
        P(),
    )
    out_specs = P("groups", None, "lat", None)

    def body(rhs, azimuthal, arrangement, polar, *matrices):
        slots, nlat, waves = polar.shape
        lat_dev = nlat // lax.axis_size("lat")
        fits = (
            slots % SUBLANES == 0
            and waves % LANES == 0
            and lat_dev % 2 == 0
            and 2 * rhs.shape[0] * rhs.shape[1] == LANES
            and rhs.shape[0] > 2
            and slots // SUBLANES > EARLY
            and lax.axis_size("lat") % NEAR == 0
            and lax.axis_size("lat") & (lax.axis_size("lat") - 1) == 0
        )
        form = per_device if fits else per_device_plain
        return form(rhs, azimuthal, arrangement, polar, *matrices)

    return jax.shard_map(
        body, mesh=mesh, in_specs=in_specs, out_specs=out_specs, check_vma=False
    )
```

```python
import functools
import jax
import jax.numpy as jnp
from jax import lax
from jax.experimental import pallas as pl
from jax.experimental.pallas import tpu as pltpu
from jax.sharding import PartitionSpec as P

NLON = 2560
LANES = 128
SUBLANES = 8
GROUP = 2
VMEM_MIB = 40
EARLY = 2
NEAR = 4

full_circle_radians = 6.283185307179586


def wave_table(azimuthal_number_list, nlon):
    longitude = jnp.arange(nlon, dtype=jnp.int32)
    coupled_product = azimuthal_number_list[:, None] * longitude[None, :] % nlon
    phase_angle = coupled_product.astype(jnp.float32) * (full_circle_radians / nlon)
    weight = jnp.where(azimuthal_number_list == 0, 1.0, 2.0).astype(jnp.float32)[:, None]
    return jnp.stack([weight * jnp.cos(phase_angle), -weight * jnp.sin(phase_angle)], 0).astype(
        jnp.bfloat16
    )


def implicit_update_quantities(rhs, position_labels, forward, back, celerity, thermal):
    offsets = jnp.arange(rhs.shape[-1], dtype=jnp.int32)
    total_n = position_labels[:, None] + offsets[None, :]
    inside = total_n < rhs.shape[-1]
    degree = total_n.astype(jnp.float32)
    laplace_eigen = degree * (degree + 1.0)
    high = lax.Precision.HIGHEST
    modal_part = jnp.einsum("ml,lcsk->mcsk", forward, rhs[0], precision=high)
    damped = modal_part / (1.0 + celerity[:, None, None, None] * laplace_eigen)
    divergence = jnp.einsum("kp,phli->khli", back, damped, precision=high)
    temperature = rhs[1] - jnp.einsum("kp,phli->khli", thermal, divergence, precision=high)
    pile = jnp.concatenate([divergence[None], temperature[None], rhs[2:]], 0)
    return jnp.where(inside, pile, jnp.zeros_like(pile)).astype(jnp.bfloat16)


def per_device_plain(rhs, azimuthal, arrangement, polar, forward, back, celerity, thermal):
    fields, levels = rhs.shape[:2]
    slots, nlat, waves = polar.shape
    lat_dev = nlat // lax.axis_size("lat")
    labels = lax.dynamic_slice_in_dim(azimuthal, lax.axis_index("lat") * slots, slots)
    coeffs = implicit_update_quantities(rhs, labels, forward, back, celerity, thermal)
    rows = fields * levels
    natural = jnp.einsum(
        "rsk,slk->rsl",
        coeffs.reshape(rows * 2, slots, waves),
        polar,
        preferred_element_type=jnp.float32,
    )
    fourier = jnp.take(natural, arrangement, axis=2).astype(jnp.bfloat16)
    fourier = fourier.reshape(rows, 2, slots, nlat)
    grid_out = jnp.einsum(
        "icsr,csj->irj",
        lax.all_to_all(fourier, "lat", split_axis=3, concat_axis=2, tiled=True),
        wave_table(azimuthal, NLON),
        preferred_element_type=jnp.float32,
    ).astype(jnp.bfloat16)
    return grid_out.reshape(fields, levels, lat_dev, NLON)


def legendre_kernel(
    *refs, levels, begin, steps, near, outs, carried, carry
):
    refs = list(refs)
    sources = [refs.pop(0) for _ in range(6)]
    rhs_hbm, polar_hbm = refs.pop(0), refs.pop(0)
    given = [refs.pop(0) for _ in range(2 * carried)]
    out_hbms = [refs.pop(0) for _ in range(outs)]
    taken = [refs.pop(0) for _ in range(2 * carry)]
    scalars = [refs.pop(0) for _ in range(6)]
    rhs_buf, polar_buf, nat_one, nat_two, pad_one, pad_two, stage_ref = refs[:7]
    scalar_sem, load_sem, out_sem = refs[7:]
    azim_ref, arr_ref, *matrices = scalars

    small = [
        pltpu.make_async_copy(src, dst, scalar_sem.at[i])
        for i, (src, dst) in enumerate(zip(sources, scalars))
    ]
    for copy in small:
        copy.start()

    def load(step, targets):
        at = pl.ds((begin + step) * SUBLANES, SUBLANES)
        solved = pl.ds(0, 4 * levels)
        others = pl.ds(4 * levels, rhs_hbm.shape[0] - 4 * levels)
        copies = [
            pltpu.make_async_copy(
                rhs_hbm.at[rows, at, :], targets[0].at[rows], load_sem.at[step, i]
            )
            for i, rows in enumerate((solved, others))
        ]
        copies.append(pltpu.make_async_copy(polar_hbm.at[at], targets[1], load_sem.at[step, 2]))
        for copy in copies:
            copy.start()
        return copies

    blocks, loads, stores = {}, {}, []
    for step in range(steps):
        own = step - carried
        blocks[step] = (rhs_buf.at[own], polar_buf.at[own]) if own >= 0 else tuple(given)
    if carry:
        blocks[steps] = tuple(taken)
    for step in range(carried, min(carried + 2, steps)):
        loads[step] = load(step, blocks[step])

    def await_loads(step, begin, end):
        for copy in loads.get(step, ())[begin:end]:
            copy.wait()

    def arrive(step):
        await_loads(step, 0, 3 if carried else 1)
        after = step + 2
        if after in blocks and after not in loads:
            loads[after] = load(after, blocks[after])

    def prepare(step):
        pad = (pad_one, pad_two)[step % 2]
        late = None if carried else functools.partial(await_loads, step, 1, 2)
        yield from update_parts(
            azim_ref, matrices, blocks[step][0], pad, begin + step, levels, late
        )

    def finish(step):
        pad, nat = ((pad_one, nat_one), (pad_two, nat_two))[step % 2]
        outputs = [stage_ref.at[step, g] for g in range(outs)]
        if not carried:
            await_loads(step, 2, 3)
        yield from product_parts(
            azim_ref, arr_ref, blocks[step][1], pad, nat, outputs, begin + step, near
        )
        for g in range(outs):
            stores.append(
                pltpu.make_async_copy(
                    stage_ref.at[step, g], out_hbms[g].at[:, step], out_sem.at[step, g]
                )
            )
            stores[-1].start()

    for copy in small:
        copy.wait()
    arrive(0)
    for _ in prepare(0):
        pass
    for step in range(steps):
        following = iter(())
        if step + 1 < steps and carried:
            arrive(step + 1)
            following = prepare(step + 1)
        for part in finish(step):
            if part == SUBLANES - 1 and step + 1 < steps and not carried:
                arrive(step + 1)
                following = prepare(step + 1)
            next(following, None)
        for _ in following:
            pass
    await_loads(steps, 0, 3)
    for copy in stores:
        copy.wait()


def first_slot(azim_ref, step):
    own = azim_ref.shape[0] // lax.axis_size("lat")
    return lax.axis_index("lat") * own + step * SUBLANES


def update_parts(azim_ref, matrices, rhs_ref, pad_ref, step, levels, late):
    fwd_ref, back_ref, cel_ref, therm_ref = matrices
    rows, _, waves = rhs_ref.shape
    tiles = waves // LANES
    pitch = row_pitch()
    first = first_slot(azim_ref, step)

    def rhs(row, t):
        return rhs_ref[row, :, t * LANES : (t + 1) * LANES]

    def move(ts):
        for t in ts:
            for row in range(4 * levels, rows):
                pad_ref[t, pl.ds(row * pitch, SUBLANES), :] = rhs(row, t)

    sub = lax.broadcasted_iota(jnp.int32, (SUBLANES, LANES), 0)
    lane = lax.broadcasted_iota(jnp.int32, (SUBLANES, LANES), 1)
    label = jnp.zeros((SUBLANES, LANES), jnp.int32)
    for s in range(SUBLANES):
        label = jnp.where(sub == s, azim_ref[first + s], label)

    for group in range(0, tiles, GROUP):
        ts = list(range(group, min(group + GROUP, tiles)))
        parts = [(t, c) for t in ts for c in range(2)]
        span = range(len(parts))

        def mix(matrix, row, operand):
            acc = [matrix[row, 0] * operand[0][i] for i in span]
            for q in range(1, levels):
                acc = [acc[i] + matrix[row, q] * operand[q][i] for i in span]
            return acc

        laplace = []
        for t in ts:
            degree = (label + lane + t * LANES).astype(jnp.float32)
            laplace.append(degree * (degree + 1.0))
        x0 = [[rhs(l * 2 + c, t) for t, c in parts] for l in range(levels)]
        damped = []
        for m in range(levels):
            modal = mix(fwd_ref, m, x0)
            den = [1.0 / (1.0 + cel_ref[m] * lap) for lap in laplace]
            damped.append([modal[i] * den[i // 2] for i in span])
        div = []
        for l in range(levels):
            div.append(mix(back_ref, l, damped))
            for i, (t, c) in enumerate(parts):
                pad_ref[t, pl.ds((l * 2 + c) * pitch, SUBLANES), :] = div[l][i]
        for l in range(levels):
            response = mix(therm_ref, l, div)
            for i, (t, c) in enumerate(parts):
                row = (levels + l) * 2 + c
                pad_ref[t, pl.ds(row * pitch, SUBLANES), :] = rhs(row, t) - response[i]
        if late is None:
            move(ts)
        yield
    if late is not None:
        late()
        move(range(tiles))
        yield


def product_parts(azim_ref, arr_ref, polar_ref, pad_ref, nat_ref, out_refs, step, near):
    _, nlat, waves = polar_ref.shape
    tiles = waves // LANES
    pitch = row_pitch()
    apart = slot_pitch(nlat)
    rows = pad_ref.shape[1] // pitch
    mine = lax.axis_index("lat")
    first = first_slot(azim_ref, step)
    for s in range(SUBLANES):
        room = waves - azim_ref[first + s]
        pieces = []
        for t in range(tiles):
            piece = jnp.concatenate(
                [pad_ref[t, pl.ds(c * pitch + s, rows // 2, stride=2 * pitch), :] for c in range(2)],
                0,
            )
            k = lax.broadcasted_iota(jnp.int32, piece.shape, 1) + t * LANES
            pieces.append(jnp.where(k < room, piece, 0.0).astype(jnp.bfloat16))
        coeffs = jnp.concatenate(pieces, 1)
        product = lax.dot_general(
            polar_ref[s], coeffs, (((1,), (1,)), ((), ())), preferred_element_type=jnp.float32
        )
        nat_ref[pl.ds(s * apart, nlat), :] = product
        yield s

    half = LANES // 2
    low = lax.broadcasted_iota(jnp.int32, (SUBLANES, LANES), 1) < half
    pairs = out_refs[0].shape[1] // (2 * SUBLANES)
    for p in range(nlat // 2):
        if near and p % (nlat // 8) == 0 and p:
            yield
        d, q = divmod(p, pairs)
        at = ((mine ^ d if near else d) * pairs + q) * 2
        a = nat_ref[pl.ds(arr_ref[at], SUBLANES, stride=apart), :]
        b = nat_ref[pl.ds(arr_ref[at + 1], SUBLANES, stride=apart), :]
        real = jnp.where(low, a, pltpu.roll(b, half, 1))
        imag = jnp.where(low, pltpu.roll(a, half, 1), b)
        group, place = divmod(d, out_refs[0].shape[0])
        out_refs[group][place, pl.ds(q * 2 * SUBLANES, 2 * SUBLANES), :] = jnp.concatenate(
            [real, imag], 0
        ).astype(jnp.bfloat16)
    yield


def row_pitch():
    return SUBLANES + 1


def slot_pitch(nlat):
    return nlat + 4


def legendre(
    rhs, azimuthal, arrangement, polar, forward, back, celerity, thermal, begin, steps,
    near=0, given=(), carry=False,
):
    fields, levels = rhs.shape[:2]
    slots, nlat, waves = polar.shape
    rows = fields * levels * 2
    tiles = waves // LANES
    devices = lax.axis_size("lat")
    depth = nlat // devices * SUBLANES
    scalars = (azimuthal, arrangement, forward, back, celerity, thermal)
    group = near or devices
    outs = devices // group
    carried = len(given) // 2
    hbm = pl.BlockSpec(memory_space=pltpu.HBM)
    vmem = pl.BlockSpec(memory_space=pltpu.VMEM)
    rhs_block, polar_block = (rows, SUBLANES, waves), (SUBLANES, nlat, waves)
    next_blocks = [
        jax.ShapeDtypeStruct(rhs_block, rhs.dtype),
        jax.ShapeDtypeStruct(polar_block, polar.dtype),
    ]
    own = steps - carried
    return pl.pallas_call(
        functools.partial(
            legendre_kernel, levels=levels, begin=begin, steps=steps, near=near, outs=outs,
            carried=carried, carry=int(carry),
        ),
        in_specs=[hbm] * (len(scalars) + 2) + [vmem] * len(given),
        out_specs=[hbm] * outs + [vmem, vmem] * carry,
        out_shape=[jax.ShapeDtypeStruct((group, steps, depth, LANES), jnp.bfloat16)] * outs
        + next_blocks * carry,
        scratch_shapes=[pltpu.SMEM(a.shape, a.dtype) for a in scalars]
        + [
            pltpu.VMEM((own, *rhs_block), rhs.dtype),
            pltpu.VMEM((own, *polar_block), polar.dtype),
        ]
        + [pltpu.VMEM((SUBLANES * slot_pitch(nlat), LANES), jnp.float32)] * 2
        + [pltpu.VMEM((tiles, rows * row_pitch(), LANES), jnp.float32)] * 2
        + [
            pltpu.VMEM((steps, outs, group, depth, LANES), jnp.bfloat16),
            pltpu.SemaphoreType.DMA((len(scalars),)),
            pltpu.SemaphoreType.DMA((steps + 1, 3)),
            pltpu.SemaphoreType.DMA((steps, outs)),
        ],
        compiler_params=pltpu.CompilerParams(vmem_limit_bytes=VMEM_MIB * 1024 * 1024),
        name="legendre",
    )(
        *(pltpu.with_memory_space_constraint(a, pltpu.HBM) for a in scalars),
        pltpu.with_memory_space_constraint(rhs.reshape(rows, slots, waves), pltpu.HBM),
        pltpu.with_memory_space_constraint(polar, pltpu.HBM),
        *(pltpu.with_memory_space_constraint(a, pltpu.VMEM) for a in given),
    )


def table_rows(m, cos_ref, sin_ref, nlon):
    blocks = nlon // LANES
    lane = lax.broadcasted_iota(jnp.int32, m.shape, 1)
    unit = full_circle_radians / nlon
    fine = ((m * lane) % nlon).astype(jnp.float32) * unit
    coarse = ((m * lane) % blocks).astype(jnp.float32) * (unit * LANES)
    weight = jnp.where(m == 0, 1.0, 2.0)
    cos_fine = weight * jnp.cos(fine)
    sin_fine = weight * jnp.sin(fine)
    cos_coarse = jnp.cos(coarse)
    sin_coarse = jnp.sin(coarse)
    for b in range(blocks // 2 + 1):
        cc = cos_coarse[:, b : b + 1]
        sc = sin_coarse[:, b : b + 1]
        at = slice(b * LANES, (b + 1) * LANES)
        cos_ref[:, at] = (cos_fine * cc - sin_fine * sc).astype(jnp.bfloat16)
        if b < blocks // 2:
            sin_ref[:, at] = (-(sin_fine * cc + cos_fine * sc)).astype(jnp.bfloat16)


def table_kernel(azim_ref, *refs, nlon, early, near):
    step = pl.program_id(0)
    mine = lax.axis_index("lat")
    devices = azim_ref.shape[0]
    groups = devices // near
    ones, others = [], []
    for i in range(2):
        d = 2 * step + i
        ones.append(azim_ref[mine ^ (d % groups * near + d // groups), :early])
        others.append(azim_ref[d, early:])
    table_rows(jnp.concatenate(ones, 0), refs[0], refs[1], nlon)
    table_rows(jnp.concatenate(others, 0), refs[2], refs[3], nlon)


def tables(azimuthal, devices, early, near):
    slots = azimuthal.shape[0] // devices
    half = NLON // 2
    spread = jnp.broadcast_to(azimuthal.reshape(devices, slots, 1), (devices, slots, LANES))
    widths = (half + LANES, half) * 2
    counts = (early, early, slots - early, slots - early)
    return pl.pallas_call(
        functools.partial(table_kernel, nlon=NLON, early=early, near=near),
        grid=(devices // 2,),
        in_specs=[pl.BlockSpec(memory_space=pltpu.VMEM)],
        out_specs=[pl.BlockSpec((2 * n, w), lambda d: (d, 0)) for n, w in zip(counts, widths)],
        out_shape=[
            jax.ShapeDtypeStruct((devices * n, w), jnp.bfloat16) for n, w in zip(counts, widths)
        ],
        compiler_params=pltpu.CompilerParams(vmem_limit_bytes=16 * 1024 * 1024),
        name="tables",
    )(spread)


def turn(x, real_ref, imag_ref, p, at):
    rows = x.astype(jnp.float32)
    count = rows.shape[0] * rows.shape[1] * SUBLANES
    for c, ref in enumerate((real_ref, imag_ref)):
        part = rows[:, :, c * SUBLANES : (c + 1) * SUBLANES].reshape(count, LANES)
        ref[pl.ds(p * LANES, LANES), pl.ds(at, count)] = part.astype(jnp.bfloat16).T


def turn_kernel(*refs):
    *parts, real_ref, imag_ref = refs
    for p in range(parts[0].shape[2]):
        turn(jnp.concatenate([ref[:, :, p] for ref in parts], 0), real_ref, imag_ref, p, 0)


def split_pairs(x, lat_dev):
    return x.reshape(*x.shape[:2], lat_dev // 2, 2 * SUBLANES, LANES)


def turned(early, lat_dev):
    parts = [split_pairs(x, lat_dev) for x in early]
    depth = sum(x.shape[0] * x.shape[1] * SUBLANES for x in early)
    vmem = pl.BlockSpec(memory_space=pltpu.VMEM)
    return pl.pallas_call(
        turn_kernel,
        in_specs=[vmem] * len(parts),
        out_specs=[vmem] * 2,
        out_shape=[jax.ShapeDtypeStruct((lat_dev * LANES // 2, depth), jnp.bfloat16)] * 2,
        compiler_params=pltpu.CompilerParams(vmem_limit_bytes=16 * 1024 * 1024),
        name="turn",
    )(*parts)


def grid_kernel(
    *refs, fields, lat_dev, block
):
    early_refs, late_ref, tables, out_hbm = refs[:2], refs[2], refs[3:7], refs[7]
    cos_ref, sin_ref, real_ref, imag_ref, out_ref, load_sem, out_sem = refs[8:]
    width = sin_ref.shape[1]
    early = tables[0].shape[0]
    nlon = 2 * width
    half = LANES // 2
    levels = half // fields
    order = list(range(width // block))[::-1]

    def span(i):
        return pl.ds(i * block, block)

    def load(i, columns, which):
        copies = []
        for n in which:
            ref = (cos_ref, sin_ref)[n % 2]
            rows = pl.ds(n // 2 * early, tables[n].shape[0])
            copies.append(
                pltpu.make_async_copy(
                    tables[n].at[:, columns], ref.at[rows, columns], load_sem.at[i, n]
                )
            )
            copies[-1].start()
        return copies

    tail = pl.ds(width, LANES)
    ends = load(len(order), tail, (0, 2))
    loads = {i: load(i, span(i), range(4)) for i in order}

    real_ref[:, :early] = early_refs[0][...]
    imag_ref[:, :early] = early_refs[1][...]
    for p in range(lat_dev // 2):
        turn(late_ref[:, :, p], real_ref, imag_ref, p, early)

    lane = lax.broadcasted_iota(jnp.int32, (lat_dev * half, LANES), 1)
    mirror = (LANES - lane) % LANES
    for copy in ends:
        copy.wait()
    after = jnp.dot(real_ref[...], cos_ref[:, tail], preferred_element_type=jnp.float32)
    stores = []
    for n, i in enumerate(order):
        for copy in loads[i]:
            copy.wait()
        even = jnp.dot(real_ref[...], cos_ref[:, span(i)], preferred_element_type=jnp.float32)
        odd = jnp.dot(imag_ref[...], sin_ref[:, span(i)], preferred_element_type=jnp.float32)
        near = even + odd
        far = even - odd
        tiles = block // LANES
        parts = [far[:, t * LANES : (t + 1) * LANES] for t in range(tiles)] + [after]
        flipped = [
            jnp.where(lane == 0, parts[t + 1], jnp.take_along_axis(parts[t], mirror, axis=1))
            for t in range(tiles)
        ]
        after = parts[0]
        for q, value in enumerate((near, jnp.concatenate(flipped[::-1], 1))):
            for r in range(lat_dev):
                for f in range(fields):
                    row = r * half + f * levels
                    out_ref[n, q, f, r] = value[row : row + levels].astype(jnp.bfloat16)
            start = i * block if q == 0 else nlon - (i + 1) * block
            stores.append(
                pltpu.make_async_copy(
                    out_ref.at[n, q], out_hbm.at[:, :, :, pl.ds(start, block)], out_sem.at[n, q]
                )
            )
            stores[-1].start()
    for copy in stores:
        copy.wait()


def grid_product(early, late, tabs, lat_dev, fields, block=256):
    width = tabs[1].shape[1]
    depth = tabs[1].shape[0] + tabs[3].shape[0]
    half = LANES // 2
    levels = half // fields
    count = width // block
    parts = [*early, split_pairs(late, lat_dev)]
    hbm = pl.BlockSpec(memory_space=pltpu.HBM)
    out = pl.pallas_call(
        functools.partial(grid_kernel, fields=fields, lat_dev=lat_dev, block=block),
        in_specs=[pl.BlockSpec(memory_space=pltpu.VMEM)] * len(parts) + [hbm] * len(tabs),
        out_specs=hbm,
        out_shape=jax.ShapeDtypeStruct((fields, lat_dev, levels, 2 * width), jnp.bfloat16),
        scratch_shapes=[
            pltpu.VMEM((depth, width + LANES), jnp.bfloat16),
            pltpu.VMEM((depth, width), jnp.bfloat16),
            pltpu.VMEM((lat_dev * half, depth), jnp.bfloat16),
            pltpu.VMEM((lat_dev * half, depth), jnp.bfloat16),
            pltpu.VMEM((count, 2, fields, lat_dev, levels, block), jnp.bfloat16),
            pltpu.SemaphoreType.DMA((count + 1, len(tabs))),
            pltpu.SemaphoreType.DMA((count, 2)),
        ],
        compiler_params=pltpu.CompilerParams(vmem_limit_bytes=40 * 1024 * 1024),
        name="grid_product",
    )(*parts, *(pltpu.with_memory_space_constraint(a, pltpu.HBM) for a in tabs))
    return jnp.swapaxes(out, 1, 2)


def per_device(rhs, azimuthal, arrangement, polar, forward, back, celerity, thermal):
    fields = rhs.shape[0]
    slots, nlat, _ = polar.shape
    devices = lax.axis_size("lat")
    lat_dev = nlat // devices
    steps = slots // SUBLANES
    operands = (rhs, azimuthal, arrangement, polar, forward, back, celerity, thermal)

    def swap(x, distance):
        return lax.ppermute(x, "lat", [(d, d ^ distance) for d in range(devices)])

    *mine, next_rhs, next_polar = legendre(*operands, 0, EARLY, NEAR, carry=True)
    got = [mine[0]]
    for g in range(1, devices // NEAR):
        got.append(swap(mine[g], g * NEAR))
    (packed,) = legendre(
        *operands, EARLY, steps - EARLY, given=(next_rhs, next_polar)
    )
    late = lax.all_to_all(packed, "lat", split_axis=0, concat_axis=0, tiled=True)
    early = []
    for j in range(NEAR):
        part = jnp.concatenate([x[j : j + 1] for x in got], 0)
        early.append(swap(part, j) if j else part)
    early = turned(early, lat_dev)
    tabs = tables(azimuthal, devices, EARLY * SUBLANES, NEAR)
    return grid_product(early, late, tabs, lat_dev, fields)


def solution(mesh):
    in_specs = (
        P("groups", None, None, "lat", None),
        P(),
        P(),
        P("lat", None, None),
        P(),
        P(),
        P(),
        P(),
    )
    out_specs = P("groups", None, "lat", None)

    def body(rhs, azimuthal, arrangement, polar, *matrices):
        slots, nlat, waves = polar.shape
        lat_dev = nlat // lax.axis_size("lat")
        fits = (
            slots % SUBLANES == 0
            and waves % LANES == 0
            and lat_dev % 2 == 0
            and 2 * rhs.shape[0] * rhs.shape[1] == LANES
            and rhs.shape[0] > 2
            and slots // SUBLANES > EARLY
            and lax.axis_size("lat") % NEAR == 0
            and lax.axis_size("lat") & (lax.axis_size("lat") - 1) == 0
        )
        form = per_device if fits else per_device_plain
        return form(rhs, azimuthal, arrangement, polar, *matrices)

    return jax.shard_map(
        body, mesh=mesh, in_specs=in_specs, out_specs=out_specs, check_vma=False
    )
```

```python
import functools
import jax
import jax.numpy as jnp
from jax import lax
from jax.experimental import pallas as pl
from jax.experimental.pallas import tpu as pltpu
from jax.sharding import PartitionSpec as P

NLON = 2560
LANES = 128
SUBLANES = 8
GROUP = 3
VMEM_MIB = 40
EARLY = 2
NEAR = 4

full_circle_radians = 6.283185307179586


def wave_table(azimuthal_number_list, nlon):
    longitude = jnp.arange(nlon, dtype=jnp.int32)
    coupled_product = azimuthal_number_list[:, None] * longitude[None, :] % nlon
    phase_angle = coupled_product.astype(jnp.float32) * (full_circle_radians / nlon)
    weight = jnp.where(azimuthal_number_list == 0, 1.0, 2.0).astype(jnp.float32)[:, None]
    return jnp.stack([weight * jnp.cos(phase_angle), -weight * jnp.sin(phase_angle)], 0).astype(
        jnp.bfloat16
    )


def implicit_update_quantities(rhs, position_labels, forward, back, celerity, thermal):
    offsets = jnp.arange(rhs.shape[-1], dtype=jnp.int32)
    total_n = position_labels[:, None] + offsets[None, :]
    inside = total_n < rhs.shape[-1]
    degree = total_n.astype(jnp.float32)
    laplace_eigen = degree * (degree + 1.0)
    high = lax.Precision.HIGHEST
    modal_part = jnp.einsum("ml,lcsk->mcsk", forward, rhs[0], precision=high)
    damped = modal_part / (1.0 + celerity[:, None, None, None] * laplace_eigen)
    divergence = jnp.einsum("kp,phli->khli", back, damped, precision=high)
    temperature = rhs[1] - jnp.einsum("kp,phli->khli", thermal, divergence, precision=high)
    pile = jnp.concatenate([divergence[None], temperature[None], rhs[2:]], 0)
    return jnp.where(inside, pile, jnp.zeros_like(pile)).astype(jnp.bfloat16)


def per_device_plain(rhs, azimuthal, arrangement, polar, forward, back, celerity, thermal):
    fields, levels = rhs.shape[:2]
    slots, nlat, waves = polar.shape
    lat_dev = nlat // lax.axis_size("lat")
    labels = lax.dynamic_slice_in_dim(azimuthal, lax.axis_index("lat") * slots, slots)
    coeffs = implicit_update_quantities(rhs, labels, forward, back, celerity, thermal)
    rows = fields * levels
    natural = jnp.einsum(
        "rsk,slk->rsl",
        coeffs.reshape(rows * 2, slots, waves),
        polar,
        preferred_element_type=jnp.float32,
    )
    fourier = jnp.take(natural, arrangement, axis=2).astype(jnp.bfloat16)
    fourier = fourier.reshape(rows, 2, slots, nlat)
    grid_out = jnp.einsum(
        "icsr,csj->irj",
        lax.all_to_all(fourier, "lat", split_axis=3, concat_axis=2, tiled=True),
        wave_table(azimuthal, NLON),
        preferred_element_type=jnp.float32,
    ).astype(jnp.bfloat16)
    return grid_out.reshape(fields, levels, lat_dev, NLON)


def legendre_kernel(
    *refs, levels, begin, steps, near, outs, carried, carry
):
    refs = list(refs)
    sources = [refs.pop(0) for _ in range(6)]
    rhs_hbm, polar_hbm = refs.pop(0), refs.pop(0)
    given = [refs.pop(0) for _ in range(2 * carried)]
    out_hbms = [refs.pop(0) for _ in range(outs)]
    taken = [refs.pop(0) for _ in range(2 * carry)]
    scalars = [refs.pop(0) for _ in range(6)]
    rhs_buf, polar_buf, nat_one, nat_two, pad_one, pad_two, stage_ref = refs[:7]
    scalar_sem, load_sem, out_sem = refs[7:]
    azim_ref, arr_ref, *matrices = scalars

    small = [
        pltpu.make_async_copy(src, dst, scalar_sem.at[i])
        for i, (src, dst) in enumerate(zip(sources, scalars))
    ]
    for copy in small:
        copy.start()

    def load(step, targets):
        at = pl.ds((begin + step) * SUBLANES, SUBLANES)
        solved = pl.ds(0, 4 * levels)
        others = pl.ds(4 * levels, rhs_hbm.shape[0] - 4 * levels)
        copies = [
            pltpu.make_async_copy(
                rhs_hbm.at[rows, at, :], targets[0].at[rows], load_sem.at[step, i]
            )
            for i, rows in enumerate((solved, others))
        ]
        copies.append(pltpu.make_async_copy(polar_hbm.at[at], targets[1], load_sem.at[step, 2]))
        for copy in copies:
            copy.start()
        return copies

    blocks, loads, stores = {}, {}, []
    for step in range(steps):
        own = step - carried
        blocks[step] = (rhs_buf.at[own], polar_buf.at[own]) if own >= 0 else tuple(given)
    if carry:
        blocks[steps] = tuple(taken)
    for step in range(carried, min(carried + 2, steps)):
        loads[step] = load(step, blocks[step])

    def await_loads(step, begin, end):
        for copy in loads.get(step, ())[begin:end]:
            copy.wait()

    def arrive(step):
        await_loads(step, 0, 3 if carried else 1)
        after = step + 2
        if after in blocks and after not in loads:
            loads[after] = load(after, blocks[after])

    def prepare(step):
        pad = (pad_one, pad_two)[step % 2]
        late = None if carried else functools.partial(await_loads, step, 1, 2)
        yield from update_parts(
            azim_ref, matrices, blocks[step][0], pad, begin + step, levels, late
        )

    def finish(step):
        pad, nat = ((pad_one, nat_one), (pad_two, nat_two))[step % 2]
        outputs = [stage_ref.at[step, g] for g in range(outs)]
        if not carried:
            await_loads(step, 2, 3)
        yield from product_parts(
            azim_ref, arr_ref, blocks[step][1], pad, nat, outputs, begin + step, near
        )
        for g in range(outs):
            stores.append(
                pltpu.make_async_copy(
                    stage_ref.at[step, g], out_hbms[g].at[:, step], out_sem.at[step, g]
                )
            )
            stores[-1].start()

    for copy in small:
        copy.wait()
    arrive(0)
    for _ in prepare(0):
        pass
    for step in range(steps):
        following = iter(())
        if step + 1 < steps and carried:
            arrive(step + 1)
            following = prepare(step + 1)
        for part in finish(step):
            if part == SUBLANES - 1 and step + 1 < steps and not carried:
                arrive(step + 1)
                following = prepare(step + 1)
            next(following, None)
        for _ in following:
            pass
    await_loads(steps, 0, 3)
    for copy in stores:
        copy.wait()


def first_slot(azim_ref, step):
    own = azim_ref.shape[0] // lax.axis_size("lat")
    return lax.axis_index("lat") * own + step * SUBLANES


def update_parts(azim_ref, matrices, rhs_ref, pad_ref, step, levels, late):
    fwd_ref, back_ref, cel_ref, therm_ref = matrices
    rows, _, waves = rhs_ref.shape
    tiles = waves // LANES
    pitch = row_pitch()
    first = first_slot(azim_ref, step)

    def rhs(row, t):
        return rhs_ref[row, :, t * LANES : (t + 1) * LANES]

    def move(ts):
        for t in ts:
            for row in range(4 * levels, rows):
                pad_ref[t, pl.ds(row * pitch, SUBLANES), :] = rhs(row, t)

    sub = lax.broadcasted_iota(jnp.int32, (SUBLANES, LANES), 0)
    lane = lax.broadcasted_iota(jnp.int32, (SUBLANES, LANES), 1)
    label = jnp.zeros((SUBLANES, LANES), jnp.int32)
    for s in range(SUBLANES):
        label = jnp.where(sub == s, azim_ref[first + s], label)

    for group in range(0, tiles, GROUP):
        ts = list(range(group, min(group + GROUP, tiles)))
        parts = [(t, c) for t in ts for c in range(2)]
        span = range(len(parts))

        def mix(matrix, row, operand):
            acc = [matrix[row, 0] * operand[0][i] for i in span]
            for q in range(1, levels):
                acc = [acc[i] + matrix[row, q] * operand[q][i] for i in span]
            return acc

        laplace = []
        for t in ts:
            degree = (label + lane + t * LANES).astype(jnp.float32)
            laplace.append(degree * (degree + 1.0))
        x0 = [[rhs(l * 2 + c, t) for t, c in parts] for l in range(levels)]
        damped = []
        for m in range(levels):
            modal = mix(fwd_ref, m, x0)
            den = [1.0 / (1.0 + cel_ref[m] * lap) for lap in laplace]
            damped.append([modal[i] * den[i // 2] for i in span])
        div = []
        for l in range(levels):
            div.append(mix(back_ref, l, damped))
            for i, (t, c) in enumerate(parts):
                pad_ref[t, pl.ds((l * 2 + c) * pitch, SUBLANES), :] = div[l][i]
        for l in range(levels):
            response = mix(therm_ref, l, div)
            for i, (t, c) in enumerate(parts):
                row = (levels + l) * 2 + c
                pad_ref[t, pl.ds(row * pitch, SUBLANES), :] = rhs(row, t) - response[i]
        if late is None:
            move(ts)
        yield
    if late is not None:
        late()
        move(range(tiles))
        yield


def product_parts(azim_ref, arr_ref, polar_ref, pad_ref, nat_ref, out_refs, step, near):
    _, nlat, waves = polar_ref.shape
    tiles = waves // LANES
    pitch = row_pitch()
    apart = slot_pitch(nlat)
    rows = pad_ref.shape[1] // pitch
    mine = lax.axis_index("lat")
    first = first_slot(azim_ref, step)
    for s in range(SUBLANES):
        room = waves - azim_ref[first + s]
        pieces = []
        for t in range(tiles):
            piece = jnp.concatenate(
                [pad_ref[t, pl.ds(c * pitch + s, rows // 2, stride=2 * pitch), :] for c in range(2)],
                0,
            )
            k = lax.broadcasted_iota(jnp.int32, piece.shape, 1) + t * LANES
            pieces.append(jnp.where(k < room, piece, 0.0).astype(jnp.bfloat16))
        coeffs = jnp.concatenate(pieces, 1)
        product = lax.dot_general(
            polar_ref[s], coeffs, (((1,), (1,)), ((), ())), preferred_element_type=jnp.float32
        )
        nat_ref[pl.ds(s * apart, nlat), :] = product
        yield s

    half = LANES // 2
    low = lax.broadcasted_iota(jnp.int32, (SUBLANES, LANES), 1) < half
    pairs = out_refs[0].shape[1] // (2 * SUBLANES)
    for p in range(nlat // 2):
        if near and p % (nlat // 8) == 0 and p:
            yield
        d, q = divmod(p, pairs)
        at = ((mine ^ d if near else d) * pairs + q) * 2
        a = nat_ref[pl.ds(arr_ref[at], SUBLANES, stride=apart), :]
        b = nat_ref[pl.ds(arr_ref[at + 1], SUBLANES, stride=apart), :]
        real = jnp.where(low, a, pltpu.roll(b, half, 1))
        imag = jnp.where(low, pltpu.roll(a, half, 1), b)
        group, place = divmod(d, out_refs[0].shape[0])
        out_refs[group][place, pl.ds(q * 2 * SUBLANES, 2 * SUBLANES), :] = jnp.concatenate(
            [real, imag], 0
        ).astype(jnp.bfloat16)
    yield


def row_pitch():
    return SUBLANES + 1


def slot_pitch(nlat):
    return nlat + 4


def legendre(
    rhs, azimuthal, arrangement, polar, forward, back, celerity, thermal, begin, steps,
    near=0, given=(), carry=False,
):
    fields, levels = rhs.shape[:2]
    slots, nlat, waves = polar.shape
    rows = fields * levels * 2
    tiles = waves // LANES
    devices = lax.axis_size("lat")
    depth = nlat // devices * SUBLANES
    scalars = (azimuthal, arrangement, forward, back, celerity, thermal)
    group = near or devices
    outs = devices // group
    carried = len(given) // 2
    hbm = pl.BlockSpec(memory_space=pltpu.HBM)
    vmem = pl.BlockSpec(memory_space=pltpu.VMEM)
    rhs_block, polar_block = (rows, SUBLANES, waves), (SUBLANES, nlat, waves)
    next_blocks = [
        jax.ShapeDtypeStruct(rhs_block, rhs.dtype),
        jax.ShapeDtypeStruct(polar_block, polar.dtype),
    ]
    own = steps - carried
    return pl.pallas_call(
        functools.partial(
            legendre_kernel, levels=levels, begin=begin, steps=steps, near=near, outs=outs,
            carried=carried, carry=int(carry),
        ),
        in_specs=[hbm] * (len(scalars) + 2) + [vmem] * len(given),
        out_specs=[hbm] * outs + [vmem, vmem] * carry,
        out_shape=[jax.ShapeDtypeStruct((group, steps, depth, LANES), jnp.bfloat16)] * outs
        + next_blocks * carry,
        scratch_shapes=[pltpu.SMEM(a.shape, a.dtype) for a in scalars]
        + [
            pltpu.VMEM((own, *rhs_block), rhs.dtype),
            pltpu.VMEM((own, *polar_block), polar.dtype),
        ]
        + [pltpu.VMEM((SUBLANES * slot_pitch(nlat), LANES), jnp.float32)] * 2
        + [pltpu.VMEM((tiles, rows * row_pitch(), LANES), jnp.float32)] * 2
        + [
            pltpu.VMEM((steps, outs, group, depth, LANES), jnp.bfloat16),
            pltpu.SemaphoreType.DMA((len(scalars),)),
            pltpu.SemaphoreType.DMA((steps + 1, 3)),
            pltpu.SemaphoreType.DMA((steps, outs)),
        ],
        compiler_params=pltpu.CompilerParams(vmem_limit_bytes=VMEM_MIB * 1024 * 1024),
        name="legendre",
    )(
        *(pltpu.with_memory_space_constraint(a, pltpu.HBM) for a in scalars),
        pltpu.with_memory_space_constraint(rhs.reshape(rows, slots, waves), pltpu.HBM),
        pltpu.with_memory_space_constraint(polar, pltpu.HBM),
        *(pltpu.with_memory_space_constraint(a, pltpu.VMEM) for a in given),
    )


def table_rows(m, cos_ref, sin_ref, nlon):
    blocks = nlon // LANES
    lane = lax.broadcasted_iota(jnp.int32, m.shape, 1)
    unit = full_circle_radians / nlon
    fine = ((m * lane) % nlon).astype(jnp.float32) * unit
    coarse = ((m * lane) % blocks).astype(jnp.float32) * (unit * LANES)
    weight = jnp.where(m == 0, 1.0, 2.0)
    cos_fine = weight * jnp.cos(fine)
    sin_fine = weight * jnp.sin(fine)
    cos_coarse = jnp.cos(coarse)
    sin_coarse = jnp.sin(coarse)
    for b in range(blocks // 2 + 1):
        cc = cos_coarse[:, b : b + 1]
        sc = sin_coarse[:, b : b + 1]
        at = slice(b * LANES, (b + 1) * LANES)
        cos_ref[:, at] = (cos_fine * cc - sin_fine * sc).astype(jnp.bfloat16)
        if b < blocks // 2:
            sin_ref[:, at] = (-(sin_fine * cc + cos_fine * sc)).astype(jnp.bfloat16)


def table_kernel(azim_ref, cos_ref, sin_ref, *, nlon, early, near):
    mine = lax.axis_index("lat")
    devices, slots, _ = azim_ref.shape
    groups = devices // near
    late = slots - early

    def two(i, carry):
        ones, others = [], []
        for d in (2 * i, 2 * i + 1):
            ones.append(azim_ref[mine ^ (d % groups * near + d // groups), :early])
            others.append(azim_ref[d, early:])
        starts = (2 * early * i, devices * early + 2 * late * i)
        for m, start in zip((ones, others), starts):
            m = jnp.concatenate(m, 0)
            rows = pl.ds(pl.multiple_of(start, 2 * SUBLANES), m.shape[0])
            table_rows(m, cos_ref.at[rows], sin_ref.at[rows], nlon)
        return carry

    lax.fori_loop(0, devices // 2, two, 0)


def tables(azimuthal, devices, early, near):
    count = azimuthal.shape[0]
    slots = count // devices
    half = NLON // 2
    spread = jnp.broadcast_to(azimuthal.reshape(devices, slots, 1), (devices, slots, LANES))
    vmem = pl.BlockSpec(memory_space=pltpu.VMEM)
    return pl.pallas_call(
        functools.partial(table_kernel, nlon=NLON, early=early, near=near),
        in_specs=[vmem],
        out_specs=[vmem] * 2,
        out_shape=[
            jax.ShapeDtypeStruct((count, w), jnp.bfloat16) for w in (half + LANES, half)
        ],
        compiler_params=pltpu.CompilerParams(vmem_limit_bytes=16 * 1024 * 1024),
        name="tables",
    )(spread)


def turn(x, real_ref, imag_ref, p, at):
    rows = x.astype(jnp.float32)
    count = rows.shape[0] * rows.shape[1] * SUBLANES
    for c, ref in enumerate((real_ref, imag_ref)):
        part = rows[:, :, c * SUBLANES : (c + 1) * SUBLANES].reshape(count, LANES)
        ref[pl.ds(p * LANES, LANES), pl.ds(at, count)] = part.astype(jnp.bfloat16).T


def turn_kernel(*refs):
    *parts, real_ref, imag_ref = refs
    for p in range(parts[0].shape[2]):
        turn(jnp.concatenate([ref[:, :, p] for ref in parts], 0), real_ref, imag_ref, p, 0)


def split_pairs(x, lat_dev):
    return x.reshape(*x.shape[:2], lat_dev // 2, 2 * SUBLANES, LANES)


def turned(early, lat_dev):
    parts = [split_pairs(x, lat_dev) for x in early]
    depth = sum(x.shape[0] * x.shape[1] * SUBLANES for x in early)
    vmem = pl.BlockSpec(memory_space=pltpu.VMEM)
    return pl.pallas_call(
        turn_kernel,
        in_specs=[vmem] * len(parts),
        out_specs=[vmem] * 2,
        out_shape=[jax.ShapeDtypeStruct((lat_dev * LANES // 2, depth), jnp.bfloat16)] * 2,
        compiler_params=pltpu.CompilerParams(vmem_limit_bytes=16 * 1024 * 1024),
        name="turn",
    )(*parts)


def grid_kernel(
    *refs, fields, lat_dev, block
):
    early_refs, late_ref, cos_ref, sin_ref, out_hbm = refs[:2], *refs[2:6]
    real_ref, imag_ref, out_ref, out_sem = refs[6:]
    width = sin_ref.shape[1]
    early = early_refs[0].shape[1]
    nlon = 2 * width
    half = LANES // 2
    levels = half // fields
    order = list(range(width // block))[::-1]

    def span(i):
        return pl.ds(i * block, block)

    tail = pl.ds(width, LANES)
    real_ref[:, :early] = early_refs[0][...]
    imag_ref[:, :early] = early_refs[1][...]
    for p in range(lat_dev // 2):
        turn(late_ref[:, :, p], real_ref, imag_ref, p, early)

    lane = lax.broadcasted_iota(jnp.int32, (lat_dev * half, LANES), 1)
    mirror = (LANES - lane) % LANES
    after = jnp.dot(real_ref[...], cos_ref[:, tail], preferred_element_type=jnp.float32)
    stores = []
    for n, i in enumerate(order):
        even = jnp.dot(real_ref[...], cos_ref[:, span(i)], preferred_element_type=jnp.float32)
        odd = jnp.dot(imag_ref[...], sin_ref[:, span(i)], preferred_element_type=jnp.float32)
        near = even + odd
        far = even - odd
        tiles = block // LANES
        parts = [far[:, t * LANES : (t + 1) * LANES] for t in range(tiles)] + [after]
        flipped = [
            jnp.where(lane == 0, parts[t + 1], jnp.take_along_axis(parts[t], mirror, axis=1))
            for t in range(tiles)
        ]
        after = parts[0]
        for q, value in enumerate((near, jnp.concatenate(flipped[::-1], 1))):
            for r in range(lat_dev):
                for f in range(fields):
                    row = r * half + f * levels
                    out_ref[n, q, f, r] = value[row : row + levels].astype(jnp.bfloat16)
            start = i * block if q == 0 else nlon - (i + 1) * block
            stores.append(
                pltpu.make_async_copy(
                    out_ref.at[n, q], out_hbm.at[:, :, :, pl.ds(start, block)], out_sem.at[n, q]
                )
            )
            stores[-1].start()
    for copy in stores:
        copy.wait()


def grid_product(early, late, tabs, lat_dev, fields, block=256):
    depth, width = tabs[1].shape
    half = LANES // 2
    levels = half // fields
    count = width // block
    parts = [*early, split_pairs(late, lat_dev)]
    hbm = pl.BlockSpec(memory_space=pltpu.HBM)
    out = pl.pallas_call(
        functools.partial(grid_kernel, fields=fields, lat_dev=lat_dev, block=block),
        in_specs=[pl.BlockSpec(memory_space=pltpu.VMEM)] * (len(parts) + len(tabs)),
        out_specs=hbm,
        out_shape=jax.ShapeDtypeStruct((fields, lat_dev, levels, 2 * width), jnp.bfloat16),
        scratch_shapes=[
            pltpu.VMEM((lat_dev * half, depth), jnp.bfloat16),
            pltpu.VMEM((lat_dev * half, depth), jnp.bfloat16),
            pltpu.VMEM((count, 2, fields, lat_dev, levels, block), jnp.bfloat16),
            pltpu.SemaphoreType.DMA((count, 2)),
        ],
        compiler_params=pltpu.CompilerParams(vmem_limit_bytes=40 * 1024 * 1024),
        name="grid_product",
    )(*parts, *(pltpu.with_memory_space_constraint(a, pltpu.VMEM) for a in tabs))
    return jnp.swapaxes(out, 1, 2)


def per_device(rhs, azimuthal, arrangement, polar, forward, back, celerity, thermal):
    fields = rhs.shape[0]
    slots, nlat, _ = polar.shape
    devices = lax.axis_size("lat")
    lat_dev = nlat // devices
    steps = slots // SUBLANES
    operands = (rhs, azimuthal, arrangement, polar, forward, back, celerity, thermal)

    def swap(x, distance):
        return lax.ppermute(x, "lat", [(d, d ^ distance) for d in range(devices)])

    *mine, next_rhs, next_polar = legendre(*operands, 0, EARLY, NEAR, carry=True)
    got = [mine[0]]
    for g in range(1, devices // NEAR):
        got.append(swap(mine[g], g * NEAR))
    (packed,) = legendre(
        *operands, EARLY, steps - EARLY, given=(next_rhs, next_polar)
    )
    late = lax.all_to_all(packed, "lat", split_axis=0, concat_axis=0, tiled=True)
    early = []
    for j in range(NEAR):
        part = jnp.concatenate([x[j : j + 1] for x in got], 0)
        early.append(swap(part, j) if j else part)
    early = turned(early, lat_dev)
    tabs = tables(azimuthal, devices, EARLY * SUBLANES, NEAR)
    return grid_product(early, late, tabs, lat_dev, fields)


def solution(mesh):
    in_specs = (
        P("groups", None, None, "lat", None),
        P(),
        P(),
        P("lat", None, None),
        P(),
        P(),
        P(),
        P(),
    )
    out_specs = P("groups", None, "lat", None)

    def body(rhs, azimuthal, arrangement, polar, *matrices):
        slots, nlat, waves = polar.shape
        lat_dev = nlat // lax.axis_size("lat")
        fits = (
            slots % SUBLANES == 0
            and waves % LANES == 0
            and lat_dev % 2 == 0
            and 2 * rhs.shape[0] * rhs.shape[1] == LANES
            and rhs.shape[0] > 2
            and slots // SUBLANES > EARLY
            and lax.axis_size("lat") % NEAR == 0
            and lax.axis_size("lat") & (lax.axis_size("lat") - 1) == 0
        )
        form = per_device if fits else per_device_plain
        return form(rhs, azimuthal, arrangement, polar, *matrices)

    return jax.shard_map(
        body, mesh=mesh, in_specs=in_specs, out_specs=out_specs, check_vma=False
    )
```
